32 devices in a mesh: gx: 4 (over y, x), gy: 2 (over core), gz: 4 (over z).
Axes of the slice: x: 2, y: 2, z: 4, core: 2. Of those that a mesh axis runs over, the one named last changes fastest.
Arguments:
- patches: bfloat16 [512, 6144], P(('gz', 'gx'), 'gy'), may hold values from -6 to 6
- modality: int32 [512], P(('gz', 'gx')), may hold values from 0 to 2
- gains: float32 [3, 6144], P(None, 'gy'), may hold values from 0.1 to 1.9
- biases: float32 [3, 6144], P(None, 'gy'), may hold values from -3 to 3
- weights: bfloat16 [3, 6144, 3072], P(None, ('gy', 'gz'), 'gx'), may hold values from -0.078125 to 0.078125
- segments: int32 [4, 128], P('gz'), may hold values from 0 to 3, never falling along the last dimension, each value on 1 to 64 neighbouring positions
- cotangent: bfloat16 [512, 3072], P(('gz', 'gy'), 'gx'), may hold values from -6 to 6
Outputs:
- attended: bfloat16 [512, 3072], P(('gz', 'gy'), 'gx')
- patch_gradient: float32 [512, 6144], P(('gz', 'gx'), 'gy')
The draws below stay inside these ranges and needn't reach their ends.
Inputs may be any that keep to these rules, and one draw needn't show every extreme that they name: `segments`: within each pack the segment ids never fall, and each segment holds at most half of 128 patches.
All inputs are finite; a program needn't handle non-finite values.
Results may differ from the reference program's by a relative error of at most 0.02.
Values may be sent and summed in bfloat16 or wider, within the bound.
A program may use at most 64 MiB of HBM per device.

```python
import math
import jax
import jax.numpy as jnp
import numpy as np
from jax import lax

MODEL_WIDTH = 6144
HEADS = 24
HEAD_DIM = 128
TOK_BLOCK = 128
MODS = 3
SEGS = 4
ATT = 3072
PACKS = 4
TOKENS = 512
N_GY = 2


def plant(entries, key, smallest, largest):
    longest = entries.shape.index(max(entries.shape))
    spots = []
    for shift in (0, 1):
        where = [jax.random.randint(jax.random.fold_in(key, axis), (), 0, length) for axis, length in enumerate(entries.shape)]
        where[longest] = (where[longest] + shift) % entries.shape[longest]
        spots.append(tuple(where))
    return entries.at[spots[0]].set(smallest).at[spots[1]].set(largest)


def steps_of(stream_key, extent, split, smallest, high):
    level, own = 1.0, jax.random.fold_in(stream_key, 6)
    for dim, shards_of in split:
        heights = jnp.exp(jax.random.uniform(jax.random.fold_in(own, dim), (shards_of,), jnp.float32, smallest / len(split), high / len(split)))
        level = level * jnp.repeat(heights, extent[dim] // shards_of).reshape([-1 if axis == dim else 1 for axis in range(len(extent))])
    return level


def length_profile(amount, total, limit, lean):
    portions = [(1 << 20) // math.isqrt(grade ** lean) + 1 for grade in range(2, amount + 1)]
    surplus, holding = total - limit - (amount - 1), [1] * (amount - 1)
    while surplus > 0:
        movable = [i for i in range(amount - 1) if holding[i] < limit]
        whole, left = sum([portions[i] for i in movable]), surplus
        for i in movable:
            more = min(limit - holding[i], max(1, left * portions[i] // whole), surplus)
            holding[i] = holding[i] + more
            surplus = surplus - more
    return np.array([limit] + holding)


def ragged_sizes(key, amount, total, most, lean):
    if amount == 2:
        one = jax.random.randint(key, (), max(1, total - most), min(most, total - 1) + 1)
        return jnp.stack([one, total - one])
    tallies = jnp.asarray(length_profile(amount, total, most, lean), jnp.int32)
    couples = (amount - 1) // 2
    donor, taker = tallies[1:1 + 2 * couples:2], tallies[2:2 + 2 * couples:2]
    room = jnp.minimum(donor - 1, most - taker)
    passed = jax.random.randint(jax.random.fold_in(key, 1), (couples,), 0, 1 << 20) % (room + 1)
    tallies = tallies.at[1:1 + 2 * couples:2].set(donor - passed).at[2:2 + 2 * couples:2].set(taker + passed)
    return tallies[jax.random.permutation(jax.random.fold_in(key, 2), amount)]


def bell_draw(key, shape, deviation, bound, cuts=(), held_as=jnp.bfloat16):
    array = jax.random.normal(key, shape, jnp.float32) * deviation
    if len(cuts) > 0:
        array = steps_of(key, shape, cuts, -0.22, 0.18) * array
    return jnp.clip(array, min=-bound, max=bound).astype(held_as)


def setup_inputs(seed: int = 0) -> dict:
    key_of = jax.random.split(jax.random.key(seed), 8)
    patches = bell_draw(key_of[0], (TOKENS, MODEL_WIDTH), 1.0, 6.0, ((0, 16), (1, 2)))
    modality = plant(jax.random.randint(key_of[1], (TOKENS,), 0, MODS), jax.random.fold_in(key_of[1], 1), 0, MODS - 1).astype(jnp.int32)
    gains = jnp.clip(1.0 + 0.18 * jax.random.normal(key_of[2], (MODS, MODEL_WIDTH), jnp.float32), 0.1, 1.9)
    biases = bell_draw(key_of[3], (MODS, MODEL_WIDTH), 0.5, 3.0, ((1, 2),), jnp.float32)
    weights = bell_draw(key_of[4], (3, MODEL_WIDTH, ATT), MODEL_WIDTH ** -0.5, 0.078125, ((1, 8), (2, 4)))
    segments = jax.vmap(lambda own: jnp.searchsorted(jnp.cumsum(ragged_sizes(own, SEGS, TOK_BLOCK, TOK_BLOCK // 2, 1)), jnp.arange(TOK_BLOCK), side="right"))(jax.random.split(key_of[5], PACKS)).reshape((PACKS, TOK_BLOCK)).astype(jnp.int32)
    cotangent = bell_draw(key_of[6], (TOKENS, ATT), 1.0, 6.0, ((0, 8), (1, 4)))
    return dict(patches=patches, modality=modality, gains=gains, biases=biases, weights=weights, segments=segments, cotangent=cotangent)


EPS = 1e-06

def pack_attention(inputs):
    queries, keys, values, segment, upstream = inputs
    scaling = HEAD_DIM ** (-0.5)
    hp = lax.Precision.HIGHEST
    scores = jnp.einsum('qhd,khd->hqk', queries.astype(jnp.float32), keys.astype(jnp.float32), precision=hp) * scaling
    allowed = segment[:, None] == segment[None, :]
    exponent = jnp.where(allowed[None], jnp.exp(scores), 0.0)
    probs = exponent / lax.optimization_barrier(jnp.sum(exponent, -1, keepdims=True))
    probs_b = probs.astype(jnp.bfloat16)
    attended = jnp.einsum('hqk,khd->qhd', probs_b.astype(jnp.float32), values.astype(jnp.float32), precision=hp).astype(jnp.bfloat16)
    upstream_f = upstream.astype(jnp.float32)
    dprobs = jnp.einsum('qhd,khd->hqk', upstream_f, values.astype(jnp.float32), precision=hp)
    dscores = (probs * (dprobs - lax.optimization_barrier(jnp.sum(probs * dprobs, -1, keepdims=True))) * scaling).astype(jnp.bfloat16)
    dqueries = jnp.einsum('hqk,khd->qhd', dscores.astype(jnp.float32), keys.astype(jnp.float32), precision=hp).astype(jnp.bfloat16)
    group = TOK_BLOCK // N_GY
    head_count = queries.shape[1]
    dscore_groups = dscores.astype(jnp.float32).reshape(head_count, N_GY, group, TOK_BLOCK)
    prob_groups = probs_b.astype(jnp.float32).reshape(head_count, N_GY, group, TOK_BLOCK)
    query_groups = queries.astype(jnp.float32).reshape(N_GY, group, head_count, HEAD_DIM)
    upstream_groups = upstream_f.reshape(N_GY, group, head_count, HEAD_DIM)
    key_parts = jnp.einsum('hgqk,gqhd->gkhd', dscore_groups, query_groups, precision=hp)
    value_parts = jnp.einsum('hgqk,gqhd->gkhd', prob_groups, upstream_groups, precision=hp)
    key_parts = lax.optimization_barrier(key_parts.astype(jnp.bfloat16)).astype(jnp.float32)
    value_parts = lax.optimization_barrier(value_parts.astype(jnp.bfloat16)).astype(jnp.float32)
    dkeys = lax.optimization_barrier(jnp.sum(key_parts, 0)).astype(jnp.bfloat16)
    dvalues = lax.optimization_barrier(jnp.sum(value_parts, 0)).astype(jnp.bfloat16)
    return (attended, dqueries, dkeys, dvalues)

def reference(patches, modality, gains, biases, weights, segments, cotangent):
    values_f = patches.astype(jnp.float32)
    average = lax.optimization_barrier(jnp.mean(values_f, -1, keepdims=True))
    mean_removed = values_f - average
    variance = lax.optimization_barrier(jnp.mean(mean_removed * mean_removed, -1, keepdims=True))
    inverse_deviation = 1.0 / jnp.sqrt(variance + EPS)
    standardized_input = mean_removed * inverse_deviation
    gain_per_row = gains[modality]
    bias_per_row = biases[modality]
    layer_normalized = (standardized_input * gain_per_row + bias_per_row).astype(jnp.bfloat16)
    width_block = MODEL_WIDTH // N_GY
    columns = HEADS * HEAD_DIM
    projected = []
    for which in range(3):
        totals = jnp.zeros((TOKENS, columns), jnp.float32)
        for blocks in range(N_GY):
            lower = blocks * width_block
            product = jnp.dot(layer_normalized[:, lower:lower + width_block], weights[which, lower:lower + width_block, :], preferred_element_type=jnp.float32)
            totals = totals + lax.optimization_barrier(product.astype(jnp.bfloat16)).astype(jnp.float32)
        projected.append(totals.astype(jnp.bfloat16).reshape(PACKS, TOK_BLOCK, HEADS, HEAD_DIM))
    upstream = cotangent.reshape(PACKS, TOK_BLOCK, HEADS, HEAD_DIM)
    attended, dqueries, dkeys, dvalues = lax.map(pack_attention, (projected[0], projected[1], projected[2], segments, upstream))
    attended = attended.reshape(TOKENS, columns)
    dnormed = jnp.zeros((TOKENS, MODEL_WIDTH), jnp.float32)
    for which, grads in enumerate((dqueries, dkeys, dvalues)):
        dnormed = dnormed + jnp.dot(grads.reshape(TOKENS, columns), weights[which].T, preferred_element_type=jnp.float32)
    normalized_gradient = dnormed * gain_per_row
    patch_gradient = inverse_deviation * (normalized_gradient - lax.optimization_barrier(jnp.mean(normalized_gradient, -1, keepdims=True)) - standardized_input * lax.optimization_barrier(jnp.mean(normalized_gradient * standardized_input, -1, keepdims=True)))
    return (attended, patch_gradient)
```

```python
import jax
import jax.numpy as jnp
from jax import lax
from jax.sharding import PartitionSpec as P

MODEL_WIDTH = 6144
HEAD_DIM = 128


EPS = 1e-06


def sum_over_width(totals):
    return lax.psum((totals[0], totals[1]), "gy")


def split_sum(partial_value):
    return lax.psum(partial_value, "gy").astype(jnp.float32)


def on_device(patches, modality, gains, biases, weights, segments, cotangent):
    values_f = patches.astype(jnp.float32)
    totals, squares = sum_over_width((jnp.sum(values_f, -1), jnp.sum(values_f * values_f, -1)))
    average = totals / MODEL_WIDTH
    variance = squares / MODEL_WIDTH - average * average
    mean_removed = values_f - average[:, None]
    inverse_deviation = lax.rsqrt(variance + EPS)[:, None]
    standardized_input = mean_removed * inverse_deviation
    levels = jnp.arange(gains.shape[0], dtype=jnp.int32)
    chosen = (modality[:, None] == levels[None, :])[:, :, None]
    gain_per_row = jnp.sum(jnp.where(chosen, gains[None], 0.0), 1)
    bias_per_row = jnp.sum(jnp.where(chosen, biases[None], 0.0), 1)
    layer_normalized = (standardized_input * gain_per_row + bias_per_row).astype(jnp.bfloat16)
    full_weights = lax.all_gather(weights, "gz", axis=1, tiled=True)
    partial_value = jnp.einsum(
        "rd,kdc->rkc",
        lax.all_gather(layer_normalized, "gx", axis=0, tiled=True),
        full_weights,
        preferred_element_type=jnp.float32,
    ).astype(jnp.bfloat16)
    pack_rows = partial_value.shape[0]
    own_rows = pack_rows // lax.axis_size("gy")
    offset = lax.axis_index("gy") * own_rows
    projected = split_sum(partial_value).astype(jnp.bfloat16)
    queries = lax.dynamic_slice_in_dim(projected[:, 0], offset, own_rows, 0)
    keys, values = (projected[:, 1], projected[:, 2])
    columns = full_weights.shape[2]
    head_count = columns // HEAD_DIM
    queries = queries.reshape(own_rows, head_count, HEAD_DIM)
    keys = keys.reshape(pack_rows, head_count, HEAD_DIM)
    values = values.reshape(pack_rows, head_count, HEAD_DIM)
    segment = segments[0]
    segment_query = lax.dynamic_slice_in_dim(segment, offset, own_rows, 0)
    allowed = (segment_query[:, None] == segment[None, :])[None]
    scaling = HEAD_DIM ** (-0.5)
    scores = jnp.einsum("qhd,khd->hqk", queries, keys, preferred_element_type=jnp.float32) * scaling
    exponent = jnp.where(allowed, jnp.exp(scores), 0.0)
    probs = exponent / jnp.sum(exponent, -1, keepdims=True)
    probs_b = probs.astype(jnp.bfloat16)
    attended = (
        jnp.einsum("hqk,khd->qhd", probs_b, values, preferred_element_type=jnp.float32)
        .astype(jnp.bfloat16)
        .reshape(own_rows, columns)
    )
    upstream = cotangent.reshape(own_rows, head_count, HEAD_DIM)
    dprobs = jnp.einsum("qhd,khd->hqk", upstream, values, preferred_element_type=jnp.float32)
    dvalues = jnp.einsum("hqk,qhd->khd", probs_b, upstream, preferred_element_type=jnp.float32)
    dscores = (probs * (dprobs - jnp.sum(probs * dprobs, -1, keepdims=True)) * scaling).astype(
        jnp.bfloat16
    )
    dqueries = jnp.einsum("hqk,khd->qhd", dscores, keys, preferred_element_type=jnp.float32)
    dkeys = jnp.einsum("hqk,qhd->khd", dscores, queries, preferred_element_type=jnp.float32)
    query_block = lax.dynamic_update_slice_in_dim(
        jnp.zeros((pack_rows, head_count, HEAD_DIM), jnp.float32), dqueries, offset, 0
    )
    stacked = (
        jnp.stack([query_block, dkeys, dvalues], 1)
        .reshape(pack_rows, 3, columns)
        .astype(jnp.bfloat16)
    )
    grad_proj = split_sum(stacked).astype(jnp.bfloat16)
    dnormed = lax.psum_scatter(
        jnp.einsum("rkc,kdc->rd", grad_proj, full_weights, preferred_element_type=jnp.float32),
        "gx",
        scatter_dimension=0,
        tiled=True,
    )
    normalized_gradient = dnormed * gain_per_row
    gradient_row_sum, weighted_row_sum = sum_over_width(
        (jnp.sum(normalized_gradient, -1), jnp.sum(normalized_gradient * standardized_input, -1))
    )
    patch_gradient = inverse_deviation * (
        normalized_gradient
        - gradient_row_sum[:, None] / MODEL_WIDTH
        - standardized_input * (weighted_row_sum[:, None] / MODEL_WIDTH)
    )
    return (attended, patch_gradient)


def stationary(patches, modality, gains, biases, weights, segments, cotangent):
    packs, parts, groups = lax.axis_size("gz"), lax.axis_size("gy"), lax.axis_size("gx")
    values_f = patches.astype(jnp.float32)
    rows, width = values_f.shape
    mine = jnp.mean(values_f, -1)
    spread = jnp.sum((values_f - mine[:, None]) ** 2, -1)
    both = lax.all_gather(jnp.stack([mine, spread]), "gy")
    average = jnp.mean(both[:, 0], 0)
    variance = (jnp.sum(both[:, 1], 0) + width * jnp.sum((both[:, 0] - average) ** 2, 0)) / MODEL_WIDTH
    inverse = lax.rsqrt(variance + EPS)[:, None]
    xhat = (values_f - average[:, None]) * inverse
    levels = jnp.arange(gains.shape[0], dtype=jnp.int32)
    chosen = (modality[:, None] == levels[None, :])[:, :, None]
    gain = jnp.sum(jnp.where(chosen, gains[None], 0.0), 1)
    bias = jnp.sum(jnp.where(chosen, biases[None], 0.0), 1)
    normed = (xhat * gain + bias).astype(jnp.bfloat16)
    block, columns = weights.shape[1:]
    share = columns // parts
    heads = share // HEAD_DIM
    moved = lax.all_to_all(normed.reshape(rows, packs, block), "gz", 1, 0, tiled=True)
    moved = moved.reshape(packs, rows, block)
    moved = lax.all_gather(moved, "gx", axis=1, tiled=True)
    length = rows * groups
    partial_value = jnp.einsum("prd,kdc->prkc", moved, weights, preferred_element_type=jnp.float32)
    partial_value = partial_value.astype(jnp.bfloat16).reshape(packs, length, 3, parts, share)
    partial_value = partial_value.transpose(0, 3, 1, 2, 4).reshape(packs * parts * length, 3 * share)
    projected = lax.psum_scatter(partial_value, ("gz", "gy"), scatter_dimension=0, tiled=True)
    projected = projected.reshape(length, 3, heads, HEAD_DIM)
    queries, keys, values = projected[:, 0], projected[:, 1], projected[:, 2]
    up = lax.all_to_all(cotangent, "gy", 1, 0, tiled=True).reshape(length, heads, HEAD_DIM)
    segment = segments[0]
    allowed = (segment[:, None] == segment[None, :])[None]
    scaling = HEAD_DIM ** (-0.5)
    f32 = dict(preferred_element_type=jnp.float32)
    scores = jnp.einsum("qhd,khd->hqk", queries, keys, **f32) * scaling
    exponent = jnp.where(allowed, jnp.exp(scores), 0.0)
    probs = exponent / jnp.sum(exponent, -1, keepdims=True)
    probs_b = probs.astype(jnp.bfloat16)
    attended = jnp.einsum("hqk,khd->qhd", probs_b, values, **f32).astype(jnp.bfloat16)
    attended = lax.all_to_all(attended.reshape(length, share), "gy", 0, 1, tiled=True)
    dprobs = jnp.einsum("qhd,khd->hqk", up, values, **f32)
    dvalues = jnp.einsum("hqk,qhd->khd", probs_b, up, **f32)
    dscores = (probs * (dprobs - jnp.sum(probs * dprobs, -1, keepdims=True)) * scaling).astype(jnp.bfloat16)
    dqueries = jnp.einsum("hqk,khd->qhd", dscores, keys, **f32)
    dkeys = jnp.einsum("hqk,qhd->khd", dscores, queries, **f32)
    stacked = jnp.stack([dqueries, dkeys, dvalues], 1).reshape(length, 3, share).astype(jnp.bfloat16)
    grads = lax.all_gather(stacked, ("gz", "gy"), axis=0).reshape(packs, parts, length, 3, share)
    grads = grads.transpose(0, 2, 3, 1, 4).reshape(packs, length, 3, columns)
    dnormed = jnp.einsum("prkc,kdc->prd", grads, weights, **f32).astype(jnp.bfloat16)
    dnormed = lax.psum_scatter(dnormed, "gx", scatter_dimension=1, tiled=True)
    dnormed = lax.all_to_all(dnormed.reshape(packs * rows, 1, block), "gz", 0, 1, tiled=True)
    dxhat = dnormed.reshape(rows, width).astype(jnp.float32) * gain
    total, weighted = lax.psum((jnp.sum(dxhat, -1), jnp.sum(dxhat * xhat, -1)), "gy")
    gradient = inverse * (dxhat - total[:, None] / MODEL_WIDTH - xhat * (weighted[:, None] / MODEL_WIDTH))
    return (attended, gradient)


def solution(mesh):
    def body(*arrays):
        weights = arrays[4]
        split = weights.shape[2] // HEAD_DIM
        fits = split % mesh.shape["gy"] == 0 and weights.shape[1] % HEAD_DIM == 0
        return (stationary if fits else on_device)(*arrays)

    return jax.shard_map(
        body,
        mesh=mesh,
        in_specs=(
            P(("gz", "gx"), "gy"),
            P(("gz", "gx")),
            P(None, "gy"),
            P(None, "gy"),
            P(None, ("gy", "gz"), "gx"),
            P("gz", None),
            P(("gz", "gy"), "gx"),
        ),
        out_specs=(P(("gz", "gy"), "gx"), P(("gz", "gx"), "gy")),
        check_vma=False,
    )
```

```python
import functools

import jax
import jax.numpy as jnp
from jax import lax
from jax.experimental import pallas as pl
from jax.experimental.pallas import tpu as pltpu
from jax.sharding import PartitionSpec as P

MODEL_WIDTH = 6144
HEAD_DIM = 128


EPS = 1e-06


def sum_over_width(totals):
    return lax.psum((totals[0], totals[1]), "gy")


def split_sum(partial_value):
    return lax.psum(partial_value, "gy").astype(jnp.float32)


def on_device(patches, modality, gains, biases, weights, segments, cotangent):
    values_f = patches.astype(jnp.float32)
    totals, squares = sum_over_width((jnp.sum(values_f, -1), jnp.sum(values_f * values_f, -1)))
    average = totals / MODEL_WIDTH
    variance = squares / MODEL_WIDTH - average * average
    mean_removed = values_f - average[:, None]
    inverse_deviation = lax.rsqrt(variance + EPS)[:, None]
    standardized_input = mean_removed * inverse_deviation
    levels = jnp.arange(gains.shape[0], dtype=jnp.int32)
    chosen = (modality[:, None] == levels[None, :])[:, :, None]
    gain_per_row = jnp.sum(jnp.where(chosen, gains[None], 0.0), 1)
    bias_per_row = jnp.sum(jnp.where(chosen, biases[None], 0.0), 1)
    layer_normalized = (standardized_input * gain_per_row + bias_per_row).astype(jnp.bfloat16)
    full_weights = lax.all_gather(weights, "gz", axis=1, tiled=True)
    partial_value = jnp.einsum(
        "rd,kdc->rkc",
        lax.all_gather(layer_normalized, "gx", axis=0, tiled=True),
        full_weights,
        preferred_element_type=jnp.float32,
    ).astype(jnp.bfloat16)
    pack_rows = partial_value.shape[0]
    own_rows = pack_rows // lax.axis_size("gy")
    offset = lax.axis_index("gy") * own_rows
    projected = split_sum(partial_value).astype(jnp.bfloat16)
    queries = lax.dynamic_slice_in_dim(projected[:, 0], offset, own_rows, 0)
    keys, values = (projected[:, 1], projected[:, 2])
    columns = full_weights.shape[2]
    head_count = columns // HEAD_DIM
    queries = queries.reshape(own_rows, head_count, HEAD_DIM)
    keys = keys.reshape(pack_rows, head_count, HEAD_DIM)
    values = values.reshape(pack_rows, head_count, HEAD_DIM)
    segment = segments[0]
    segment_query = lax.dynamic_slice_in_dim(segment, offset, own_rows, 0)
    allowed = (segment_query[:, None] == segment[None, :])[None]
    scaling = HEAD_DIM ** (-0.5)
    scores = jnp.einsum("qhd,khd->hqk", queries, keys, preferred_element_type=jnp.float32) * scaling
    exponent = jnp.where(allowed, jnp.exp(scores), 0.0)
    probs = exponent / jnp.sum(exponent, -1, keepdims=True)
    probs_b = probs.astype(jnp.bfloat16)
    attended = (
        jnp.einsum("hqk,khd->qhd", probs_b, values, preferred_element_type=jnp.float32)
        .astype(jnp.bfloat16)
        .reshape(own_rows, columns)
    )
    upstream = cotangent.reshape(own_rows, head_count, HEAD_DIM)
    dprobs = jnp.einsum("qhd,khd->hqk", upstream, values, preferred_element_type=jnp.float32)
    dvalues = jnp.einsum("hqk,qhd->khd", probs_b, upstream, preferred_element_type=jnp.float32)
    dscores = (probs * (dprobs - jnp.sum(probs * dprobs, -1, keepdims=True)) * scaling).astype(
        jnp.bfloat16
    )
    dqueries = jnp.einsum("hqk,khd->qhd", dscores, keys, preferred_element_type=jnp.float32)
    dkeys = jnp.einsum("hqk,qhd->khd", dscores, queries, preferred_element_type=jnp.float32)
    query_block = lax.dynamic_update_slice_in_dim(
        jnp.zeros((pack_rows, head_count, HEAD_DIM), jnp.float32), dqueries, offset, 0
    )
    stacked = (
        jnp.stack([query_block, dkeys, dvalues], 1)
        .reshape(pack_rows, 3, columns)
        .astype(jnp.bfloat16)
    )
    grad_proj = split_sum(stacked).astype(jnp.bfloat16)
    dnormed = lax.psum_scatter(
        jnp.einsum("rkc,kdc->rd", grad_proj, full_weights, preferred_element_type=jnp.float32),
        "gx",
        scatter_dimension=0,
        tiled=True,
    )
    normalized_gradient = dnormed * gain_per_row
    gradient_row_sum, weighted_row_sum = sum_over_width(
        (jnp.sum(normalized_gradient, -1), jnp.sum(normalized_gradient * standardized_input, -1))
    )
    patch_gradient = inverse_deviation * (
        normalized_gradient
        - gradient_row_sum[:, None] / MODEL_WIDTH
        - standardized_input * (weighted_row_sum[:, None] / MODEL_WIDTH)
    )
    return (attended, patch_gradient)


MESH = pl.DeviceIdType.MESH
F32 = dict(preferred_element_type=jnp.float32)


def dot(a, b, da, db):
    return lax.dot_general(a, b, (((da,), (db,)), ((), ())), **F32)


def layer(
    nx, nz, patches, modality, gains, biases, weights, segments, cotangent, attended, gradient,
    held, mixed, xhat, gain, stat_out, stat_in, normed, rows_in, part_out, part_in, grads,
    up, att_out, att_in, y_out, y_in, z_out, z_in,
    local_sem, pair_send, pair_recv, a_send, a_recv, b_send, b_recv, c_send, c_recv,
    p_send, p_recv, g_send, g_recv, h_send, h_recv, y_send, y_recv, z_send, z_recv,
):
    x, y, z = lax.axis_index("gx"), lax.axis_index("gy"), lax.axis_index("gz")
    other = 1 - y
    rows, width = patches.shape
    block, columns = weights.shape[1:]
    share = columns // 2
    length = rows * nx
    half = length // 2
    count = 2 * width
    order = (0,) + tuple(sorted(range(1, nz), key=lambda d: min(d, nz - d)))
    sends = []

    def send(source, target, send_sem, recv_sem, where):
        copy = pltpu.make_async_remote_copy(
            src_ref=source, dst_ref=target, send_sem=send_sem, recv_sem=recv_sem,
            device_id=where, device_id_type=MESH,
        )
        copy.start()
        sends.append(copy)
        return copy

    def along(axis, me, size, step):
        return {axis: lax.rem(me + step + size, size)}

    barrier = pltpu.get_barrier_semaphore()
    pl.semaphore_signal(barrier, inc=1, device_id={"gy": other}, device_id_type=MESH)
    for step in range(1, nx):
        pl.semaphore_signal(barrier, inc=1, device_id=along("gx", x, nx, step), device_id_type=MESH)
    for step in range(1, nz):
        pl.semaphore_signal(barrier, inc=1, device_id=along("gz", z, nz, step), device_id_type=MESH)
    own_columns = pl.ds(pl.multiple_of(y * share, HEAD_DIM), share)
    other_columns = pl.ds(pl.multiple_of(other * share, HEAD_DIM), share)
    keep = pltpu.make_async_copy(weights.at[:, :, own_columns], mixed.at[y], local_sem.at[0])
    keep.start()
    load = pltpu.make_async_copy(weights, held, local_sem.at[1])
    load.start()

    values = patches[...].astype(jnp.float32)
    mine = jnp.sum(values, -1, keepdims=True) / width
    spread = jnp.sum((values - mine) ** 2, -1, keepdims=True)
    lane = lax.broadcasted_iota(jnp.int32, (rows, HEAD_DIM), 1)
    stat_out[0] = jnp.where(lane == 0, mine, spread)
    pl.semaphore_wait(barrier, nx + nz - 1)
    to_pair = {"gy": other}
    first = send(stat_out.at[0], stat_in.at[0], pair_send.at[0], pair_recv.at[0], to_pair)
    swap_w = send(weights.at[:, :, other_columns], mixed.at[y], pair_send.at[1], pair_recv.at[1], to_pair)
    swap_u = send(cotangent.at[:, other_columns], up.at[y], pair_send.at[2], pair_recv.at[2], to_pair)
    up[y] = cotangent[:, own_columns]

    diagonal = lax.broadcasted_iota(jnp.int32, (rows, rows), 0) == lax.broadcasted_iota(jnp.int32, (rows, rows), 1)
    level = jnp.sum(jnp.where(diagonal, modality[...], 0), 1, keepdims=True)
    for part in range(nz):
        cols = slice(part * block, (part + 1) * block)
        chosen = jnp.zeros((rows, block), jnp.float32)
        for index in range(gains.shape[0]):
            chosen = jnp.where(level == index, gains[index:index + 1, cols], chosen)
        gain[:, cols] = chosen
    first.wait_recv()
    theirs = stat_in[0]
    their_mean, their_spread = theirs[:, 0:1], theirs[:, 1:2]
    average = (mine + their_mean) * 0.5
    variance = (spread + their_spread + (mine - their_mean) ** 2 * (width * 0.5)) / count
    inverse = lax.rsqrt(variance + EPS)
    for part in range(nz):
        cols = slice(part * block, (part + 1) * block)
        offset = jnp.zeros((rows, block), jnp.float32)
        for index in range(biases.shape[0]):
            offset = jnp.where(level == index, biases[index:index + 1, cols], offset)
        standard = (patches[:, cols].astype(jnp.float32) - average) * inverse
        xhat[:, cols] = standard
        normed[part] = (standard * gain[:, cols] + offset).astype(jnp.bfloat16)

    place = pltpu.make_async_copy(normed.at[z], rows_in.at[y, 0, x], local_sem.at[2])
    place.start()
    arrive_a, arrive_b, arrive_c = {}, {}, {}
    for e in range(1, nx):
        arrive_b[0, e] = send(normed.at[z], rows_in.at[y, 0, x], b_send.at[0, e], b_recv.at[0, e], along("gx", x, nx, e))
    for d in order[1:]:
        arrive_a[d] = send(
            normed.at[lax.rem(z + d, nz)], rows_in.at[y, d, x], a_send.at[d], a_recv.at[d], along("gz", z, nz, d)
        )
    for d in order[1:]:
        arrive_a[d].wait_recv()
        for e in range(1, nx):
            arrive_b[d, e] = send(
                rows_in.at[y, d, x], rows_in.at[y, d, x], b_send.at[d, e], b_recv.at[d, e], along("gx", x, nx, e)
            )
    place.wait()
    keep.wait()
    arrive_p = {}

    def project(d):
        arrive_c[d].wait_recv()
        for k in range(3):
            total = jnp.zeros((length, share), jnp.float32)
            for g in range(2):
                total = total + dot(rows_in[g, d].reshape(length, block), mixed[g, k], 1, 0)
            part_out[d, :, k * share:(k + 1) * share] = total.astype(jnp.bfloat16)
        if d:
            arrive_p[d] = send(part_out.at[d], part_in.at[d], p_send.at[d], p_recv.at[d], along("gz", z, nz, -d))

    last = None
    for d in order:
        for e in range(1, nx):
            arrive_b[d, e].wait_recv()
        arrive_c[d] = send(rows_in.at[y, d], rows_in.at[y, d], c_send.at[d], c_recv.at[d], to_pair)
        if last is None:
            swap_w.wait_recv()
        else:
            project(last)
        last = d
    project(last)

    marks = segments[...]
    diagonal = lax.broadcasted_iota(jnp.int32, (length, length), 0) == lax.broadcasted_iota(
        jnp.int32, (length, length), 1
    )
    allowed = jnp.sum(jnp.where(diagonal, marks, 0), 1, keepdims=True) == marks
    scaling = HEAD_DIM ** (-0.5)
    load.wait()
    swap_u.wait_recv()
    for d in order[1:]:
        arrive_p[d].wait_recv()
    for h in range(share // HEAD_DIM):
        taken = []
        for k in range(3):
            cols = slice(k * share + h * HEAD_DIM, k * share + (h + 1) * HEAD_DIM)
            total = part_out[0, :, cols].astype(jnp.float32)
            for d in order[1:]:
                total = total + part_in[d, :, cols].astype(jnp.float32)
            taken.append(total.astype(jnp.bfloat16))
        query, key, value = taken
        here = slice(h * HEAD_DIM, (h + 1) * HEAD_DIM)
        above = up[:, :, here].reshape(length, HEAD_DIM)
        exponent = jnp.where(allowed, jnp.exp(dot(query, key, 1, 1) * scaling), 0.0)
        probs = exponent / jnp.sum(exponent, -1, keepdims=True)
        probs_b = probs.astype(jnp.bfloat16)
        att = dot(probs_b, value, 1, 0).astype(jnp.bfloat16)
        att_out[:, :, here] = att.reshape(2, half, HEAD_DIM)
        dprobs = dot(above, value, 1, 1)
        dscores = probs * (dprobs - jnp.sum(probs * dprobs, -1, keepdims=True)) * scaling
        dscores_b = dscores.astype(jnp.bfloat16)
        found = (
            dot(dscores_b, key, 1, 0),
            dot(dscores_b, query, 0, 0),
            dot(probs_b, above, 0, 0),
        )
        for k in range(3):
            cols = slice(k * share + h * HEAD_DIM, k * share + (h + 1) * HEAD_DIM)
            grads[0, y, :, cols] = found[k].astype(jnp.bfloat16)

    arrive_g, arrive_h, arrive_y, arrive_z = {}, {}, {}, {}
    for d in order[1:]:
        arrive_g[d] = send(grads.at[0, y], grads.at[d, y], g_send.at[d], g_recv.at[d], along("gz", z, nz, d))
    arrive_h[0] = send(grads.at[0, y], grads.at[0, y], h_send.at[0], h_recv.at[0], to_pair)
    swap_a = send(att_out.at[other], att_in, pair_send.at[3], pair_recv.at[3], to_pair)

    def back(d):
        arrive_h[d].wait_recv()
        total = jnp.zeros((length, block), jnp.float32)
        for k in range(3):
            for g in range(2):
                total = total + dot(
                    grads[d, g, :, k * share:(k + 1) * share], held[k, :, g * share:(g + 1) * share], 1, 1
                )
        y_out[d] = total.astype(jnp.bfloat16).reshape(nx, rows, block)
        for e in range(1, nx):
            arrive_y[d, e] = send(
                y_out.at[d, lax.rem(x + e, nx)], y_in.at[d, e], y_send.at[d, e], y_recv.at[d, e], along("gx", x, nx, e)
            )

    def collect(d):
        total = y_out[d, x].astype(jnp.float32)
        for e in range(1, nx):
            arrive_y[d, e].wait_recv()
            total = total + y_in[d, e].astype(jnp.float32)
        if d:
            z_out[d] = total.astype(jnp.bfloat16)
            arrive_z[d] = send(z_out.at[d], z_in.at[d], z_send.at[d], z_recv.at[d], along("gz", z, nz, -d))
        else:
            z_out[0] = total.astype(jnp.bfloat16)

    back(0)
    attended[:, own_columns] = att_out[y]
    swap_a.wait_recv()
    attended[:, other_columns] = att_in[...]
    last = 0
    for d in order[1:]:
        arrive_g[d].wait_recv()
        arrive_h[d] = send(grads.at[d, y], grads.at[d, y], h_send.at[d], h_recv.at[d], to_pair)
        collect(last)
        back(d)
        last = d
    collect(last)

    plain = jnp.zeros((rows, 1), jnp.float32)
    weighted = jnp.zeros((rows, 1), jnp.float32)
    for d in order:
        if d:
            arrive_z[d].wait_recv()
        cols = pl.ds(pl.multiple_of(lax.rem(z + d, nz) * block, HEAD_DIM), block)
        dxhat = (z_in[d] if d else z_out[0]).astype(jnp.float32) * gain[:, cols]
        gain[:, cols] = dxhat
        plain = plain + jnp.sum(dxhat, -1, keepdims=True)
        weighted = weighted + jnp.sum(dxhat * xhat[:, cols], -1, keepdims=True)
    stat_out[1] = jnp.where(lane == 0, plain, weighted)
    second = send(stat_out.at[1], stat_in.at[1], pair_send.at[4], pair_recv.at[4], to_pair)
    second.wait_recv()
    theirs = stat_in[1]
    plain = (plain + theirs[:, 0:1]) / count
    weighted = (weighted + theirs[:, 1:2]) / count
    for part in range(nz):
        cols = slice(part * block, (part + 1) * block)
        gradient[:, cols] = inverse * (gain[:, cols] - plain - xhat[:, cols] * weighted)
    for copy in sends:
        copy.wait_send()


def in_one_kernel(nx, nz, patches, modality, gains, biases, weights, segments, cotangent):
    rows, width = patches.shape
    block, columns = weights.shape[1:]
    share, length = columns // 2, rows * nx
    half = length // 2
    bf16, f32 = jnp.bfloat16, jnp.float32
    dma = pltpu.SemaphoreType.DMA
    vmem = pl.BlockSpec(memory_space=pltpu.VMEM)
    in_specs = [vmem] * 7
    in_specs[4] = pl.BlockSpec(memory_space=pl.ANY)
    return pl.pallas_call(
        functools.partial(layer, nx, nz),
        out_shape=(
            jax.ShapeDtypeStruct((half, columns), bf16),
            jax.ShapeDtypeStruct((rows, width), f32),
        ),
        in_specs=in_specs,
        out_specs=(vmem, vmem),
        scratch_shapes=[
            pltpu.VMEM((3, block, columns), bf16),
            pltpu.VMEM((2, 3, block, share), bf16),
            pltpu.VMEM((rows, width), f32),
            pltpu.VMEM((rows, width), f32),
            pltpu.VMEM((2, rows, HEAD_DIM), f32),
            pltpu.VMEM((2, rows, HEAD_DIM), f32),
            pltpu.VMEM((nz, rows, block), bf16),
            pltpu.VMEM((2, nz, nx, rows, block), bf16),
            pltpu.VMEM((nz, length, 3 * share), bf16),
            pltpu.VMEM((nz, length, 3 * share), bf16),
            pltpu.VMEM((nz, 2, length, 3 * share), bf16),
            pltpu.VMEM((2, half, share), bf16),
            pltpu.VMEM((2, half, share), bf16),
            pltpu.VMEM((half, share), bf16),
            pltpu.VMEM((nz, nx, rows, block), bf16),
            pltpu.VMEM((nz, nx, rows, block), bf16),
            pltpu.VMEM((nz, rows, block), bf16),
            pltpu.VMEM((nz, rows, block), bf16),
            dma((3,)), dma((5,)), dma((5,)), dma((nz,)), dma((nz,)), dma((nz, nx)), dma((nz, nx)),
            dma((nz,)), dma((nz,)), dma((nz,)), dma((nz,)), dma((nz,)), dma((nz,)), dma((nz,)), dma((nz,)),
            dma((nz, nx)), dma((nz, nx)), dma((nz,)), dma((nz,)),
        ],
        compiler_params=pltpu.CompilerParams(
            collective_id=0, has_side_effects=True, vmem_limit_bytes=56 << 20
        ),
    )(patches, modality.reshape(1, rows), gains, biases, weights, segments, cotangent)


def solution(mesh):
    nx, ny, nz = mesh.shape["gx"], mesh.shape["gy"], mesh.shape["gz"]

    def body(*arrays):
        patches, weights, segments = arrays[0], arrays[4], arrays[5]
        block, columns = weights.shape[1:]
        fits = (
            ny == 2
            and nx > 1
            and nz > 1
            and columns % (2 * HEAD_DIM) == 0
            and block % HEAD_DIM == 0
            and patches.shape[0] % 16 == 0
            and segments.shape == (1, patches.shape[0] * nx)
            and 2 * patches.shape[1] == MODEL_WIDTH
        )
        return in_one_kernel(nx, nz, *arrays) if fits else on_device(*arrays)

    return jax.shard_map(
        body,
        mesh=mesh,
        in_specs=(
            P(("gz", "gx"), "gy"),
            P(("gz", "gx")),
            P(None, "gy"),
            P(None, "gy"),
            P(None, ("gy", "gz"), "gx"),
            P("gz", None),
            P(("gz", "gy"), "gx"),
        ),
        out_specs=(P(("gz", "gy"), "gx"), P(("gz", "gx"), "gy")),
        check_vma=False,
    )
```

```python
import functools

import jax
import jax.numpy as jnp
from jax import lax
from jax.experimental import pallas as pl
from jax.experimental.pallas import tpu as pltpu
from jax.sharding import PartitionSpec as P

MODEL_WIDTH = 6144
HEAD_DIM = 128


EPS = 1e-06


def sum_over_width(totals):
    return lax.psum((totals[0], totals[1]), "gy")


def split_sum(partial_value):
    return lax.psum(partial_value, "gy").astype(jnp.float32)


def on_device(patches, modality, gains, biases, weights, segments, cotangent):
    values_f = patches.astype(jnp.float32)
    totals, squares = sum_over_width((jnp.sum(values_f, -1), jnp.sum(values_f * values_f, -1)))
    average = totals / MODEL_WIDTH
    variance = squares / MODEL_WIDTH - average * average
    mean_removed = values_f - average[:, None]
    inverse_deviation = lax.rsqrt(variance + EPS)[:, None]
    standardized_input = mean_removed * inverse_deviation
    levels = jnp.arange(gains.shape[0], dtype=jnp.int32)
    chosen = (modality[:, None] == levels[None, :])[:, :, None]
    gain_per_row = jnp.sum(jnp.where(chosen, gains[None], 0.0), 1)
    bias_per_row = jnp.sum(jnp.where(chosen, biases[None], 0.0), 1)
    layer_normalized = (standardized_input * gain_per_row + bias_per_row).astype(jnp.bfloat16)
    full_weights = lax.all_gather(weights, "gz", axis=1, tiled=True)
    partial_value = jnp.einsum(
        "rd,kdc->rkc",
        lax.all_gather(layer_normalized, "gx", axis=0, tiled=True),
        full_weights,
        preferred_element_type=jnp.float32,
    ).astype(jnp.bfloat16)
    pack_rows = partial_value.shape[0]
    own_rows = pack_rows // lax.axis_size("gy")
    offset = lax.axis_index("gy") * own_rows
    projected = split_sum(partial_value).astype(jnp.bfloat16)
    queries = lax.dynamic_slice_in_dim(projected[:, 0], offset, own_rows, 0)
    keys, values = (projected[:, 1], projected[:, 2])
    columns = full_weights.shape[2]
    head_count = columns // HEAD_DIM
    queries = queries.reshape(own_rows, head_count, HEAD_DIM)
    keys = keys.reshape(pack_rows, head_count, HEAD_DIM)
    values = values.reshape(pack_rows, head_count, HEAD_DIM)
    segment = segments[0]
    segment_query = lax.dynamic_slice_in_dim(segment, offset, own_rows, 0)
    allowed = (segment_query[:, None] == segment[None, :])[None]
    scaling = HEAD_DIM ** (-0.5)
    scores = jnp.einsum("qhd,khd->hqk", queries, keys, preferred_element_type=jnp.float32) * scaling
    exponent = jnp.where(allowed, jnp.exp(scores), 0.0)
    probs = exponent / jnp.sum(exponent, -1, keepdims=True)
    probs_b = probs.astype(jnp.bfloat16)
    attended = (
        jnp.einsum("hqk,khd->qhd", probs_b, values, preferred_element_type=jnp.float32)
        .astype(jnp.bfloat16)
        .reshape(own_rows, columns)
    )
    upstream = cotangent.reshape(own_rows, head_count, HEAD_DIM)
    dprobs = jnp.einsum("qhd,khd->hqk", upstream, values, preferred_element_type=jnp.float32)
    dvalues = jnp.einsum("hqk,qhd->khd", probs_b, upstream, preferred_element_type=jnp.float32)
    dscores = (probs * (dprobs - jnp.sum(probs * dprobs, -1, keepdims=True)) * scaling).astype(
        jnp.bfloat16
    )
    dqueries = jnp.einsum("hqk,khd->qhd", dscores, keys, preferred_element_type=jnp.float32)
    dkeys = jnp.einsum("hqk,qhd->khd", dscores, queries, preferred_element_type=jnp.float32)
    query_block = lax.dynamic_update_slice_in_dim(
        jnp.zeros((pack_rows, head_count, HEAD_DIM), jnp.float32), dqueries, offset, 0
    )
    stacked = (
        jnp.stack([query_block, dkeys, dvalues], 1)
        .reshape(pack_rows, 3, columns)
        .astype(jnp.bfloat16)
    )
    grad_proj = split_sum(stacked).astype(jnp.bfloat16)
    dnormed = lax.psum_scatter(
        jnp.einsum("rkc,kdc->rd", grad_proj, full_weights, preferred_element_type=jnp.float32),
        "gx",
        scatter_dimension=0,
        tiled=True,
    )
    normalized_gradient = dnormed * gain_per_row
    gradient_row_sum, weighted_row_sum = sum_over_width(
        (jnp.sum(normalized_gradient, -1), jnp.sum(normalized_gradient * standardized_input, -1))
    )
    patch_gradient = inverse_deviation * (
        normalized_gradient
        - gradient_row_sum[:, None] / MODEL_WIDTH
        - standardized_input * (weighted_row_sum[:, None] / MODEL_WIDTH)
    )
    return (attended, patch_gradient)


MESH = pl.DeviceIdType.MESH
F32 = dict(preferred_element_type=jnp.float32)


def dot(a, b, da, db):
    return lax.dot_general(a, b, (((da,), (db,)), ((), ())), **F32)


def layer(
    nx, nz, patches, modality, gains, biases, weights, segments, cotangent, attended, gradient,
    held, mixed, xhat, gain, stat_out, stat_in, normed, rows_in, part_out, part_in, grads,
    up, att_out, att_in, y_out, y_in, z_out, z_in,
    local_sem, pair_send, pair_recv, a_send, a_recv, b_send, b_recv, c_send, c_recv,
    p_send, p_recv, g_send, g_recv, h_send, h_recv, y_send, y_recv, z_send, z_recv,
):
    x, y, z = lax.axis_index("gx"), lax.axis_index("gy"), lax.axis_index("gz")
    other = 1 - y
    rows, width = patches.shape
    block, columns = weights.shape[1:]
    share = columns // 2
    length = rows * nx
    half = length // 2
    count = 2 * width
    upper = lax.div(2 * z, nz)
    outward = 1 - 2 * upper
    at_edge = jnp.logical_or(z == 0, z == nz - 1)
    queue = [upper * i + (1 - upper) * (nz - 1 - i) for i in range(nz)]
    sends = []

    def when(condition, action):
        if condition is None:
            action()
        else:
            pl.when(condition)(action)

    def inside(index):
        return jnp.logical_and(index >= 0, index < nz)

    def send(source, target, send_sem, recv_sem, where, condition=None):
        copy = pltpu.make_async_remote_copy(
            src_ref=source, dst_ref=target, send_sem=send_sem, recv_sem=recv_sem,
            device_id=where, device_id_type=MESH,
        )
        when(condition, copy.start)
        sends.append((condition, copy))
        return copy

    def arrived(target, recv_sem, condition=None):
        copy = pltpu.make_async_remote_copy(
            src_ref=target, dst_ref=target, send_sem=local_sem.at[3], recv_sem=recv_sem,
            device_id={"gy": other}, device_id_type=MESH,
        )
        when(condition, copy.wait_recv)

    def along(axis, me, size, step):
        return {axis: lax.rem(me + step + size, size)}

    barrier = pltpu.get_barrier_semaphore()
    pl.semaphore_signal(barrier, inc=1, device_id={"gy": other}, device_id_type=MESH)
    for step in range(1, nx):
        pl.semaphore_signal(barrier, inc=1, device_id=along("gx", x, nx, step), device_id_type=MESH)
    for step in range(1, nz):
        pl.semaphore_signal(barrier, inc=1, device_id=along("gz", z, nz, step), device_id_type=MESH)
    own_columns = pl.ds(pl.multiple_of(y * share, HEAD_DIM), share)
    other_columns = pl.ds(pl.multiple_of(other * share, HEAD_DIM), share)
    keep = pltpu.make_async_copy(weights.at[:, :, own_columns], mixed.at[y], local_sem.at[0])
    keep.start()
    load = pltpu.make_async_copy(weights, held, local_sem.at[1])
    load.start()

    values = patches[...].astype(jnp.float32)
    mine = jnp.sum(values, -1, keepdims=True) / width
    spread = jnp.sum((values - mine) ** 2, -1, keepdims=True)
    lane = lax.broadcasted_iota(jnp.int32, (rows, HEAD_DIM), 1)
    stat_out[0] = jnp.where(lane == 0, mine, spread)
    pl.semaphore_wait(barrier, nx + nz - 1)
    to_pair = {"gy": other}
    first = send(stat_out.at[0], stat_in.at[0], pair_send.at[0], pair_recv.at[0], to_pair)
    swap_w = send(weights.at[:, :, other_columns], mixed.at[y], pair_send.at[1], pair_recv.at[1], to_pair)
    swap_u = send(cotangent.at[:, other_columns], up.at[y], pair_send.at[2], pair_recv.at[2], to_pair)
    up[y] = cotangent[:, own_columns]

    diagonal = lax.broadcasted_iota(jnp.int32, (rows, rows), 0) == lax.broadcasted_iota(jnp.int32, (rows, rows), 1)
    level = jnp.sum(jnp.where(diagonal, modality[...], 0), 1, keepdims=True)
    for part in range(nz):
        cols = slice(part * block, (part + 1) * block)
        chosen = jnp.zeros((rows, block), jnp.float32)
        for index in range(gains.shape[0]):
            chosen = jnp.where(level == index, gains[index:index + 1, cols], chosen)
        gain[:, cols] = chosen
    first.wait_recv()
    theirs = stat_in[0]
    their_mean, their_spread = theirs[:, 0:1], theirs[:, 1:2]
    average = (mine + their_mean) * 0.5
    variance = (spread + their_spread + (mine - their_mean) ** 2 * (width * 0.5)) / count
    inverse = lax.rsqrt(variance + EPS)
    for part in range(nz):
        cols = slice(part * block, (part + 1) * block)
        offset = jnp.zeros((rows, block), jnp.float32)
        for index in range(biases.shape[0]):
            offset = jnp.where(level == index, biases[index:index + 1, cols], offset)
        standard = (patches[:, cols].astype(jnp.float32) - average) * inverse
        xhat[:, cols] = standard
        normed[part] = (standard * gain[:, cols] + offset).astype(jnp.bfloat16)

    place = pltpu.make_async_copy(normed.at[z], rows_in.at[y, z, x], local_sem.at[2])
    place.start()
    for q in queue:
        send(
            normed.at[q], rows_in.at[y, z, x], a_send.at[q], a_recv.at[z], {"gz": q}, q != z
        )
    for e in range(1, nx):
        send(normed.at[z], rows_in.at[y, z, x], b_send.at[z, e], b_recv.at[z, e], along("gx", x, nx, e))
    for p in queue:
        arrived(rows_in.at[y, p, x], a_recv.at[p], p != z)
        for e in range(1, nx):
            send(
                rows_in.at[y, p, x], rows_in.at[y, p, x], b_send.at[p, e], b_recv.at[p, e],
                along("gx", x, nx, e), p != z,
            )
    place.wait()
    keep.wait()

    def project(p):
        arrived(rows_in.at[other, p], c_recv.at[p])
        for k in range(3):
            total = jnp.zeros((length, share), jnp.float32)
            for g in range(2):
                total = total + dot(rows_in[g, p].reshape(length, block), mixed[g, k], 1, 0)
            part_out[p, :, k * share:(k + 1) * share] = total.astype(jnp.bfloat16)
        send(
            part_out.at[p], part_in.at[upper, p], p_send.at[p], p_recv.at[upper, p],
            along("gz", z, nz, outward), jnp.logical_and(at_edge, p != z),
        )

    last = None
    for p in queue:
        for e in range(1, nx):
            arrived(rows_in.at[y, p, lax.rem(x - e + nx, nx)], b_recv.at[p, e])
        send(rows_in.at[y, p], rows_in.at[y, p], c_send.at[p], c_recv.at[p], to_pair)
        if last is None:
            swap_w.wait_recv()
        else:
            project(last)
        last = p
    project(last)

    def add_in(side, p):
        part_out[p] = (part_out[p].astype(jnp.float32) + part_in[side, p].astype(jnp.float32)).astype(jnp.bfloat16)

    for t in range(nz - 1):
        for way in (outward, -outward):
            side = lax.div(1 - way, 2)
            p = (1 - side) * (nz - 1 - t) + side * t
            relays = jnp.logical_and((p - z) * way > 0, inside(z - way))
            arrived(part_in.at[side, p], p_recv.at[side, p], relays)
            when(relays, functools.partial(add_in, side, p))
            send(
                part_out.at[p], part_in.at[side, p], p_send.at[p], p_recv.at[side, p],
                along("gz", z, nz, way), relays,
            )

    marks = segments[...]
    diagonal = lax.broadcasted_iota(jnp.int32, (length, length), 0) == lax.broadcasted_iota(
        jnp.int32, (length, length), 1
    )
    allowed = jnp.sum(jnp.where(diagonal, marks, 0), 1, keepdims=True) == marks
    scaling = HEAD_DIM ** (-0.5)
    load.wait()
    swap_u.wait_recv()
    for side, present in ((0, z > 0), (1, z < nz - 1)):
        arrived(part_in.at[side, z], p_recv.at[side, z], present)
        when(present, functools.partial(add_in, side, z))
    for h in range(share // HEAD_DIM):
        taken = []
        for k in range(3):
            cols = slice(k * share + h * HEAD_DIM, k * share + (h + 1) * HEAD_DIM)
            taken.append(part_out[z, :, cols])
        query, key, value = taken
        here = slice(h * HEAD_DIM, (h + 1) * HEAD_DIM)
        above = up[:, :, here].reshape(length, HEAD_DIM)
        exponent = jnp.where(allowed, jnp.exp(dot(query, key, 1, 1) * scaling), 0.0)
        probs = exponent / jnp.sum(exponent, -1, keepdims=True)
        probs_b = probs.astype(jnp.bfloat16)
        att = dot(probs_b, value, 1, 0).astype(jnp.bfloat16)
        att_out[:, :, here] = att.reshape(2, half, HEAD_DIM)
        dprobs = dot(above, value, 1, 1)
        dscores = probs * (dprobs - jnp.sum(probs * dprobs, -1, keepdims=True)) * scaling
        dscores_b = dscores.astype(jnp.bfloat16)
        found = (
            dot(dscores_b, key, 1, 0),
            dot(dscores_b, query, 0, 0),
            dot(probs_b, above, 0, 0),
        )
        for k in range(3):
            cols = slice(k * share + h * HEAD_DIM, k * share + (h + 1) * HEAD_DIM)
            grads[z, y, :, cols] = found[k].astype(jnp.bfloat16)

    def pass_on(p, way, condition):
        send(
            grads.at[p, y], grads.at[p, y], g_send.at[(1 - way) // 2, p], g_recv.at[p],
            along("gz", z, nz, way), jnp.logical_and(condition, inside(z + way)),
        )

    for way in (1, -1):
        pass_on(z, way, True)
    send(grads.at[z, y], grads.at[z, y], h_send.at[z], h_recv.at[z], to_pair)
    swap_a = send(att_out.at[other], att_in, pair_send.at[3], pair_recv.at[3], to_pair)

    def back(p, condition=None):
        arrived(grads.at[p, other], h_recv.at[p], condition)

        def multiply():
            total = jnp.zeros((length, block), jnp.float32)
            for k in range(3):
                for g in range(2):
                    total = total + dot(
                        grads[p, g, :, k * share:(k + 1) * share], held[k, :, g * share:(g + 1) * share], 1, 1
                    )
            y_out[p] = total.astype(jnp.bfloat16).reshape(nx, rows, block)

        when(condition, multiply)
        for e in range(1, nx):
            send(
                y_out.at[p, lax.rem(x + e, nx)], y_in.at[p, e], y_send.at[p, e], y_recv.at[p, e],
                along("gx", x, nx, e), condition,
            )

    def collect(p, condition=None):
        for e in range(1, nx):
            arrived(y_in.at[p, e], y_recv.at[p, e], condition)

        def add_up():
            total = y_out[p, x].astype(jnp.float32)
            for e in range(1, nx):
                total = total + y_in[p, e].astype(jnp.float32)
            if condition is None:
                z_in[z] = total.astype(jnp.bfloat16)
            else:
                z_out[p] = total.astype(jnp.bfloat16)

        when(condition, add_up)
        if condition is not None:
            send(z_out.at[p], z_in.at[z], z_send.at[p], z_recv.at[z], {"gz": p}, condition)

    back(z)
    attended[:, own_columns] = att_out[y]
    swap_a.wait_recv()
    attended[:, other_columns] = att_in[...]
    waiting = [(z, None)]
    for t in range(1, nz):
        found = []
        for way in (1, -1):
            p = lax.rem(z - way * t + nz, nz)
            present = inside(z - way * t)
            arrived(grads.at[p, y], g_recv.at[p], present)
            pass_on(p, way, present)
            send(grads.at[p, y], grads.at[p, y], h_send.at[p], h_recv.at[p], to_pair, present)
            found.append((p, present))
        for p, present in waiting:
            collect(p, present)
        for p, present in found:
            back(p, present)
        waiting = found
    for p, present in waiting:
        collect(p, present)

    plain = jnp.zeros((rows, 1), jnp.float32)
    weighted = jnp.zeros((rows, 1), jnp.float32)
    for part in range(nz):
        arrived(z_in.at[part], z_recv.at[part], z != part)
        cols = slice(part * block, (part + 1) * block)
        dxhat = z_in[part].astype(jnp.float32) * gain[:, cols]
        gain[:, cols] = dxhat
        plain = plain + jnp.sum(dxhat, -1, keepdims=True)
        weighted = weighted + jnp.sum(dxhat * xhat[:, cols], -1, keepdims=True)
    stat_out[1] = jnp.where(lane == 0, plain, weighted)
    second = send(stat_out.at[1], stat_in.at[1], pair_send.at[4], pair_recv.at[4], to_pair)
    second.wait_recv()
    theirs = stat_in[1]
    plain = (plain + theirs[:, 0:1]) / count
    weighted = (weighted + theirs[:, 1:2]) / count
    for part in range(nz):
        cols = slice(part * block, (part + 1) * block)
        gradient[:, cols] = inverse * (gain[:, cols] - plain - xhat[:, cols] * weighted)
    for condition, copy in sends:
        when(condition, copy.wait_send)


def in_one_kernel(nx, nz, patches, modality, gains, biases, weights, segments, cotangent):
    rows, width = patches.shape
    block, columns = weights.shape[1:]
    share, length = columns // 2, rows * nx
    half = length // 2
    bf16, f32 = jnp.bfloat16, jnp.float32
    dma = pltpu.SemaphoreType.DMA
    vmem = pl.BlockSpec(memory_space=pltpu.VMEM)
    in_specs = [vmem] * 7
    in_specs[4] = pl.BlockSpec(memory_space=pl.ANY)
    return pl.pallas_call(
        functools.partial(layer, nx, nz),
        out_shape=(
            jax.ShapeDtypeStruct((half, columns), bf16),
            jax.ShapeDtypeStruct((rows, width), f32),
        ),
        in_specs=in_specs,
        out_specs=(vmem, vmem),
        scratch_shapes=[
            pltpu.VMEM((3, block, columns), bf16),
            pltpu.VMEM((2, 3, block, share), bf16),
            pltpu.VMEM((rows, width), f32),
            pltpu.VMEM((rows, width), f32),
            pltpu.VMEM((2, rows, HEAD_DIM), f32),
            pltpu.VMEM((2, rows, HEAD_DIM), f32),
            pltpu.VMEM((nz, rows, block), bf16),
            pltpu.VMEM((2, nz, nx, rows, block), bf16),
            pltpu.VMEM((nz, length, 3 * share), bf16),
            pltpu.VMEM((2, nz, length, 3 * share), bf16),
            pltpu.VMEM((nz, 2, length, 3 * share), bf16),
            pltpu.VMEM((2, half, share), bf16),
            pltpu.VMEM((2, half, share), bf16),
            pltpu.VMEM((half, share), bf16),
            pltpu.VMEM((nz, nx, rows, block), bf16),
            pltpu.VMEM((nz, nx, rows, block), bf16),
            pltpu.VMEM((nz, rows, block), bf16),
            pltpu.VMEM((nz, rows, block), bf16),
            dma((4,)), dma((5,)), dma((5,)), dma((nz,)), dma((nz,)), dma((nz, nx)), dma((nz, nx)),
            dma((nz,)), dma((nz,)), dma((nz,)), dma((2, nz)), dma((2, nz)), dma((nz,)), dma((nz,)), dma((nz,)),
            dma((nz, nx)), dma((nz, nx)), dma((nz,)), dma((nz,)),
        ],
        compiler_params=pltpu.CompilerParams(
            collective_id=0, has_side_effects=True, vmem_limit_bytes=56 << 20
        ),
    )(patches, modality.reshape(1, rows), gains, biases, weights, segments, cotangent)


def solution(mesh):
    nx, ny, nz = mesh.shape["gx"], mesh.shape["gy"], mesh.shape["gz"]

    def body(*arrays):
        patches, weights, segments = arrays[0], arrays[4], arrays[5]
        block, columns = weights.shape[1:]
        fits = (
            ny == 2
            and nx > 1
            and nz > 1
            and columns % (2 * HEAD_DIM) == 0
            and block % HEAD_DIM == 0
            and patches.shape[0] % 16 == 0
            and segments.shape == (1, patches.shape[0] * nx)
            and 2 * patches.shape[1] == MODEL_WIDTH
        )
        return in_one_kernel(nx, nz, *arrays) if fits else on_device(*arrays)

    return jax.shard_map(
        body,
        mesh=mesh,
        in_specs=(
            P(("gz", "gx"), "gy"),
            P(("gz", "gx")),
            P(None, "gy"),
            P(None, "gy"),
            P(None, ("gy", "gz"), "gx"),
            P("gz", None),
            P(("gz", "gy"), "gx"),
        ),
        out_specs=(P(("gz", "gy"), "gx"), P(("gz", "gx"), "gy")),
        check_vma=False,
    )
```

```python
import functools

import jax
import jax.numpy as jnp
from jax import lax
from jax.experimental import pallas as pl
from jax.experimental.pallas import tpu as pltpu
from jax.sharding import PartitionSpec as P

MODEL_WIDTH = 6144
HEAD_DIM = 128


EPS = 1e-06


def sum_over_width(totals):
    return lax.psum((totals[0], totals[1]), "gy")


def split_sum(partial_value):
    return lax.psum(partial_value, "gy").astype(jnp.float32)


def on_device(patches, modality, gains, biases, weights, segments, cotangent):
    values_f = patches.astype(jnp.float32)
    totals, squares = sum_over_width((jnp.sum(values_f, -1), jnp.sum(values_f * values_f, -1)))
    average = totals / MODEL_WIDTH
    variance = squares / MODEL_WIDTH - average * average
    mean_removed = values_f - average[:, None]
    inverse_deviation = lax.rsqrt(variance + EPS)[:, None]
    standardized_input = mean_removed * inverse_deviation
    levels = jnp.arange(gains.shape[0], dtype=jnp.int32)
    chosen = (modality[:, None] == levels[None, :])[:, :, None]
    gain_per_row = jnp.sum(jnp.where(chosen, gains[None], 0.0), 1)
    bias_per_row = jnp.sum(jnp.where(chosen, biases[None], 0.0), 1)
    layer_normalized = (standardized_input * gain_per_row + bias_per_row).astype(jnp.bfloat16)
    full_weights = lax.all_gather(weights, "gz", axis=1, tiled=True)
    partial_value = jnp.einsum(
        "rd,kdc->rkc",
        lax.all_gather(layer_normalized, "gx", axis=0, tiled=True),
        full_weights,
        preferred_element_type=jnp.float32,
    ).astype(jnp.bfloat16)
    pack_rows = partial_value.shape[0]
    own_rows = pack_rows // lax.axis_size("gy")
    offset = lax.axis_index("gy") * own_rows
    projected = split_sum(partial_value).astype(jnp.bfloat16)
    queries = lax.dynamic_slice_in_dim(projected[:, 0], offset, own_rows, 0)
    keys, values = (projected[:, 1], projected[:, 2])
    columns = full_weights.shape[2]
    head_count = columns // HEAD_DIM
    queries = queries.reshape(own_rows, head_count, HEAD_DIM)
    keys = keys.reshape(pack_rows, head_count, HEAD_DIM)
    values = values.reshape(pack_rows, head_count, HEAD_DIM)
    segment = segments[0]
    segment_query = lax.dynamic_slice_in_dim(segment, offset, own_rows, 0)
    allowed = (segment_query[:, None] == segment[None, :])[None]
    scaling = HEAD_DIM ** (-0.5)
    scores = jnp.einsum("qhd,khd->hqk", queries, keys, preferred_element_type=jnp.float32) * scaling
    exponent = jnp.where(allowed, jnp.exp(scores), 0.0)
    probs = exponent / jnp.sum(exponent, -1, keepdims=True)
    probs_b = probs.astype(jnp.bfloat16)
    attended = (
        jnp.einsum("hqk,khd->qhd", probs_b, values, preferred_element_type=jnp.float32)
        .astype(jnp.bfloat16)
        .reshape(own_rows, columns)
    )
    upstream = cotangent.reshape(own_rows, head_count, HEAD_DIM)
    dprobs = jnp.einsum("qhd,khd->hqk", upstream, values, preferred_element_type=jnp.float32)
    dvalues = jnp.einsum("hqk,qhd->khd", probs_b, upstream, preferred_element_type=jnp.float32)
    dscores = (probs * (dprobs - jnp.sum(probs * dprobs, -1, keepdims=True)) * scaling).astype(
        jnp.bfloat16
    )
    dqueries = jnp.einsum("hqk,khd->qhd", dscores, keys, preferred_element_type=jnp.float32)
    dkeys = jnp.einsum("hqk,qhd->khd", dscores, queries, preferred_element_type=jnp.float32)
    query_block = lax.dynamic_update_slice_in_dim(
        jnp.zeros((pack_rows, head_count, HEAD_DIM), jnp.float32), dqueries, offset, 0
    )
    stacked = (
        jnp.stack([query_block, dkeys, dvalues], 1)
        .reshape(pack_rows, 3, columns)
        .astype(jnp.bfloat16)
    )
    grad_proj = split_sum(stacked).astype(jnp.bfloat16)
    dnormed = lax.psum_scatter(
        jnp.einsum("rkc,kdc->rd", grad_proj, full_weights, preferred_element_type=jnp.float32),
        "gx",
        scatter_dimension=0,
        tiled=True,
    )
    normalized_gradient = dnormed * gain_per_row
    gradient_row_sum, weighted_row_sum = sum_over_width(
        (jnp.sum(normalized_gradient, -1), jnp.sum(normalized_gradient * standardized_input, -1))
    )
    patch_gradient = inverse_deviation * (
        normalized_gradient
        - gradient_row_sum[:, None] / MODEL_WIDTH
        - standardized_input * (weighted_row_sum[:, None] / MODEL_WIDTH)
    )
    return (attended, patch_gradient)


MESH = pl.DeviceIdType.MESH
F32 = dict(preferred_element_type=jnp.float32)


def dot(a, b, da, db):
    return lax.dot_general(a, b, (((da,), (db,)), ((), ())), **F32)


def layer(
    nx, nz, patches, modality, gains, biases, weights, segments, cotangent, attended, gradient,
    held, mixed, xhat, gain, stat_out, stat_in, normed, rows_in, part_out, part_in, grads,
    up, att_out, att_in, y_out, y_in, z_out, z_in,
    local_sem, pair_send, pair_recv, a_send, a_recv, b_send, b_recv, c_send, c_recv,
    p_send, p_recv, g_send, g_recv, h_send, h_recv, y_send, y_recv, z_send, z_recv,
):
    x, y, z = lax.axis_index("gx"), lax.axis_index("gy"), lax.axis_index("gz")
    other = 1 - y
    rows, width = patches.shape
    block, columns = weights.shape[1:]
    share = columns // 2
    length = rows * nx
    half = length // 2
    count = 2 * width
    upper = lax.div(2 * z, nz)
    outward = 1 - 2 * upper
    at_edge = jnp.logical_or(z == 0, z == nz - 1)
    queue = [upper * i + (1 - upper) * (nz - 1 - i) for i in range(nz)]
    cuts = [(c, pl.ds(c * half, half)) for c in range(2)]
    sends = []

    def when(condition, action):
        if condition is None:
            action()
        else:
            pl.when(condition)(action)

    def inside(index):
        return jnp.logical_and(index >= 0, index < nz)

    def send(source, target, send_sem, recv_sem, where, condition=None):
        copy = pltpu.make_async_remote_copy(
            src_ref=source, dst_ref=target, send_sem=send_sem, recv_sem=recv_sem,
            device_id=where, device_id_type=MESH,
        )
        when(condition, copy.start)
        sends.append((condition, copy))
        return copy

    def arrived(target, recv_sem, condition=None):
        copy = pltpu.make_async_remote_copy(
            src_ref=target, dst_ref=target, send_sem=local_sem.at[3], recv_sem=recv_sem,
            device_id={"gy": other}, device_id_type=MESH,
        )
        when(condition, copy.wait_recv)

    def along(axis, me, size, step):
        return {axis: lax.rem(me + step + size, size)}

    barrier = pltpu.get_barrier_semaphore()
    pl.semaphore_signal(barrier, inc=1, device_id={"gy": other}, device_id_type=MESH)
    for step in range(1, nx):
        pl.semaphore_signal(barrier, inc=1, device_id=along("gx", x, nx, step), device_id_type=MESH)
    for step in range(1, nz):
        pl.semaphore_signal(barrier, inc=1, device_id=along("gz", z, nz, step), device_id_type=MESH)
    own_columns = pl.ds(pl.multiple_of(y * share, HEAD_DIM), share)
    other_columns = pl.ds(pl.multiple_of(other * share, HEAD_DIM), share)
    keep = pltpu.make_async_copy(weights.at[:, :, own_columns], mixed.at[y], local_sem.at[0])
    keep.start()
    load = pltpu.make_async_copy(weights, held, local_sem.at[1])
    load.start()

    values = patches[...].astype(jnp.float32)
    mine = jnp.sum(values, -1, keepdims=True) / width
    spread = jnp.sum((values - mine) ** 2, -1, keepdims=True)
    lane = lax.broadcasted_iota(jnp.int32, (rows, HEAD_DIM), 1)
    stat_out[0] = jnp.where(lane == 0, mine, spread)
    pl.semaphore_wait(barrier, nx + nz - 1)
    to_pair = {"gy": other}
    first = send(stat_out.at[0], stat_in.at[0], pair_send.at[0], pair_recv.at[0], to_pair)
    swap_w = send(weights.at[:, :, other_columns], mixed.at[y], pair_send.at[1], pair_recv.at[1], to_pair)
    swap_u = send(cotangent.at[:, other_columns], up.at[y], pair_send.at[2], pair_recv.at[2], to_pair)
    up[y] = cotangent[:, own_columns]

    diagonal = lax.broadcasted_iota(jnp.int32, (rows, rows), 0) == lax.broadcasted_iota(jnp.int32, (rows, rows), 1)
    level = jnp.sum(jnp.where(diagonal, modality[...], 0), 1, keepdims=True)
    for part in range(nz):
        cols = slice(part * block, (part + 1) * block)
        chosen = jnp.zeros((rows, block), jnp.float32)
        for index in range(gains.shape[0]):
            chosen = jnp.where(level == index, gains[index:index + 1, cols], chosen)
        gain[:, cols] = chosen
    first.wait_recv()
    theirs = stat_in[0]
    their_mean, their_spread = theirs[:, 0:1], theirs[:, 1:2]
    average = (mine + their_mean) * 0.5
    variance = (spread + their_spread + (mine - their_mean) ** 2 * (width * 0.5)) / count
    inverse = lax.rsqrt(variance + EPS)
    for part in range(nz):
        cols = slice(part * block, (part + 1) * block)
        offset = jnp.zeros((rows, block), jnp.float32)
        for index in range(biases.shape[0]):
            offset = jnp.where(level == index, biases[index:index + 1, cols], offset)
        standard = (patches[:, cols].astype(jnp.float32) - average) * inverse
        xhat[:, cols] = standard
        normed[part] = (standard * gain[:, cols] + offset).astype(jnp.bfloat16)

    place = pltpu.make_async_copy(normed.at[z], rows_in.at[y, z, x], local_sem.at[2])
    place.start()
    for q in queue:
        send(
            normed.at[q], rows_in.at[y, z, x], a_send.at[q], a_recv.at[z], {"gz": q}, q != z
        )
    for e in range(1, nx):
        send(normed.at[z], rows_in.at[y, z, x], b_send.at[z, e], b_recv.at[z, e], along("gx", x, nx, e))
    for p in queue:
        arrived(rows_in.at[y, p, x], a_recv.at[p], p != z)
        for e in range(1, nx):
            send(
                rows_in.at[y, p, x], rows_in.at[y, p, x], b_send.at[p, e], b_recv.at[p, e],
                along("gx", x, nx, e), p != z,
            )
    place.wait()
    keep.wait()

    def project(p):
        arrived(rows_in.at[other, p], c_recv.at[p])
        for k in range(3):
            total = jnp.zeros((length, share), jnp.float32)
            for g in range(2):
                total = total + dot(rows_in[g, p].reshape(length, block), mixed[g, k], 1, 0)
            part_out[p, :, k * share:(k + 1) * share] = total.astype(jnp.bfloat16)
        for c, cut in cuts:
            send(
                part_out.at[p, cut], part_in.at[upper, p, cut], p_send.at[p, c], p_recv.at[upper, p, c],
                along("gz", z, nz, outward), jnp.logical_and(at_edge, p != z),
            )

    last = None
    for p in queue:
        for e in range(1, nx):
            arrived(rows_in.at[y, p, lax.rem(x - e + nx, nx)], b_recv.at[p, e])
        send(rows_in.at[y, p], rows_in.at[y, p], c_send.at[p], c_recv.at[p], to_pair)
        if last is None:
            swap_w.wait_recv()
        else:
            project(last)
        last = p
    project(last)

    def add_in(side, p, cut):
        total = part_out[p, cut].astype(jnp.float32) + part_in[side, p, cut].astype(jnp.float32)
        part_out[p, cut] = total.astype(jnp.bfloat16)

    for t in range(nz - 1):
        for way in (outward, -outward):
            side = lax.div(1 - way, 2)
            p = (1 - side) * (nz - 1 - t) + side * t
            relays = jnp.logical_and((p - z) * way > 0, inside(z - way))
            for c, cut in cuts:
                arrived(part_in.at[side, p, cut], p_recv.at[side, p, c], relays)
                when(relays, functools.partial(add_in, side, p, cut))
                send(
                    part_out.at[p, cut], part_in.at[side, p, cut], p_send.at[p, c], p_recv.at[side, p, c],
                    along("gz", z, nz, way), relays,
                )

    marks = segments[...]
    diagonal = lax.broadcasted_iota(jnp.int32, (length, length), 0) == lax.broadcasted_iota(
        jnp.int32, (length, length), 1
    )
    allowed = jnp.sum(jnp.where(diagonal, marks, 0), 1, keepdims=True) == marks
    scaling = HEAD_DIM ** (-0.5)
    load.wait()
    swap_u.wait_recv()
    for side, present in ((0, z > 0), (1, z < nz - 1)):
        for c, cut in cuts:
            arrived(part_in.at[side, z, cut], p_recv.at[side, z, c], present)
            when(present, functools.partial(add_in, side, z, cut))
    for h in range(share // HEAD_DIM):
        taken = []
        for k in range(3):
            cols = slice(k * share + h * HEAD_DIM, k * share + (h + 1) * HEAD_DIM)
            taken.append(part_out[z, :, cols])
        query, key, value = taken
        here = slice(h * HEAD_DIM, (h + 1) * HEAD_DIM)
        above = up[:, :, here].reshape(length, HEAD_DIM)
        exponent = jnp.where(allowed, jnp.exp(dot(query, key, 1, 1) * scaling), 0.0)
        probs = exponent / jnp.sum(exponent, -1, keepdims=True)
        probs_b = probs.astype(jnp.bfloat16)
        att = dot(probs_b, value, 1, 0).astype(jnp.bfloat16)
        att_out[:, :, here] = att.reshape(2, half, HEAD_DIM)
        dprobs = dot(above, value, 1, 1)
        dscores = probs * (dprobs - jnp.sum(probs * dprobs, -1, keepdims=True)) * scaling
        dscores_b = dscores.astype(jnp.bfloat16)
        found = (
            dot(dscores_b, key, 1, 0),
            dot(dscores_b, query, 0, 0),
            dot(probs_b, above, 0, 0),
        )
        for k in range(3):
            cols = slice(k * share + h * HEAD_DIM, k * share + (h + 1) * HEAD_DIM)
            grads[z, y, :, cols] = found[k].astype(jnp.bfloat16)

    def pass_on(p, way, condition, c, cut):
        send(
            grads.at[p, y, cut], grads.at[p, y, cut], g_send.at[(1 - way) // 2, p, c], g_recv.at[p, c],
            along("gz", z, nz, way), jnp.logical_and(condition, inside(z + way)),
        )

    for c, cut in cuts:
        for way in (1, -1):
            pass_on(z, way, True, c, cut)
        send(grads.at[z, y, cut], grads.at[z, y, cut], h_send.at[z, c], h_recv.at[z, c], to_pair)
    swap_a = send(att_out.at[other], att_in, pair_send.at[3], pair_recv.at[3], to_pair)

    def back(p, condition=None):
        for c, cut in cuts:
            arrived(grads.at[p, other, cut], h_recv.at[p, c], condition)

        def multiply():
            total = jnp.zeros((length, block), jnp.float32)
            for k in range(3):
                for g in range(2):
                    total = total + dot(
                        grads[p, g, :, k * share:(k + 1) * share], held[k, :, g * share:(g + 1) * share], 1, 1
                    )
            y_out[p] = total.astype(jnp.bfloat16).reshape(nx, rows, block)

        when(condition, multiply)
        for e in range(1, nx):
            send(
                y_out.at[p, lax.rem(x + e, nx)], y_in.at[p, e], y_send.at[p, e], y_recv.at[p, e],
                along("gx", x, nx, e), condition,
            )

    def collect(p, condition=None):
        for e in range(1, nx):
            arrived(y_in.at[p, e], y_recv.at[p, e], condition)

        def add_up():
            total = y_out[p, x].astype(jnp.float32)
            for e in range(1, nx):
                total = total + y_in[p, e].astype(jnp.float32)
            if condition is None:
                z_in[z] = total.astype(jnp.bfloat16)
            else:
                z_out[p] = total.astype(jnp.bfloat16)

        when(condition, add_up)
        if condition is not None:
            send(z_out.at[p], z_in.at[z], z_send.at[p], z_recv.at[z], {"gz": p}, condition)

    back(z)
    attended[:, own_columns] = att_out[y]
    swap_a.wait_recv()
    attended[:, other_columns] = att_in[...]
    waiting = [(z, None)]
    for t in range(1, nz):
        found = []
        for c, cut in cuts:
            for way in (1, -1):
                p = lax.rem(z - way * t + nz, nz)
                present = inside(z - way * t)
                arrived(grads.at[p, y, cut], g_recv.at[p, c], present)
                pass_on(p, way, present, c, cut)
                send(
                    grads.at[p, y, cut], grads.at[p, y, cut], h_send.at[p, c], h_recv.at[p, c], to_pair, present
                )
                if c == 0:
                    found.append((p, present))
        for p, present in waiting:
            collect(p, present)
        for p, present in found:
            back(p, present)
        waiting = found
    for p, present in waiting:
        collect(p, present)

    plain = jnp.zeros((rows, 1), jnp.float32)
    weighted = jnp.zeros((rows, 1), jnp.float32)
    for part in range(nz):
        arrived(z_in.at[part], z_recv.at[part], z != part)
        cols = slice(part * block, (part + 1) * block)
        dxhat = z_in[part].astype(jnp.float32) * gain[:, cols]
        gain[:, cols] = dxhat
        plain = plain + jnp.sum(dxhat, -1, keepdims=True)
        weighted = weighted + jnp.sum(dxhat * xhat[:, cols], -1, keepdims=True)
    stat_out[1] = jnp.where(lane == 0, plain, weighted)
    second = send(stat_out.at[1], stat_in.at[1], pair_send.at[4], pair_recv.at[4], to_pair)
    second.wait_recv()
    theirs = stat_in[1]
    plain = (plain + theirs[:, 0:1]) / count
    weighted = (weighted + theirs[:, 1:2]) / count
    for part in range(nz):
        cols = slice(part * block, (part + 1) * block)
        gradient[:, cols] = inverse * (gain[:, cols] - plain - xhat[:, cols] * weighted)
    for condition, copy in sends:
        when(condition, copy.wait_send)


def in_one_kernel(nx, nz, patches, modality, gains, biases, weights, segments, cotangent):
    rows, width = patches.shape
    block, columns = weights.shape[1:]
    share, length = columns // 2, rows * nx
    half = length // 2
    bf16, f32 = jnp.bfloat16, jnp.float32
    dma = pltpu.SemaphoreType.DMA
    vmem = pl.BlockSpec(memory_space=pltpu.VMEM)
    in_specs = [vmem] * 7
    in_specs[4] = pl.BlockSpec(memory_space=pl.ANY)
    return pl.pallas_call(
        functools.partial(layer, nx, nz),
        out_shape=(
            jax.ShapeDtypeStruct((half, columns), bf16),
            jax.ShapeDtypeStruct((rows, width), f32),
        ),
        in_specs=in_specs,
        out_specs=(vmem, vmem),
        scratch_shapes=[
            pltpu.VMEM((3, block, columns), bf16),
            pltpu.VMEM((2, 3, block, share), bf16),
            pltpu.VMEM((rows, width), f32),
            pltpu.VMEM((rows, width), f32),
            pltpu.VMEM((2, rows, HEAD_DIM), f32),
            pltpu.VMEM((2, rows, HEAD_DIM), f32),
            pltpu.VMEM((nz, rows, block), bf16),
            pltpu.VMEM((2, nz, nx, rows, block), bf16),
            pltpu.VMEM((nz, length, 3 * share), bf16),
            pltpu.VMEM((2, nz, length, 3 * share), bf16),
            pltpu.VMEM((nz, 2, length, 3 * share), bf16),
            pltpu.VMEM((2, half, share), bf16),
            pltpu.VMEM((2, half, share), bf16),
            pltpu.VMEM((half, share), bf16),
            pltpu.VMEM((nz, nx, rows, block), bf16),
            pltpu.VMEM((nz, nx, rows, block), bf16),
            pltpu.VMEM((nz, rows, block), bf16),
            pltpu.VMEM((nz, rows, block), bf16),
            dma((4,)), dma((5,)), dma((5,)), dma((nz,)), dma((nz,)), dma((nz, nx)), dma((nz, nx)),
            dma((nz,)), dma((nz,)), dma((nz, 2)), dma((2, nz, 2)), dma((2, nz, 2)), dma((nz, 2)),
            dma((nz, 2)), dma((nz, 2)),
            dma((nz, nx)), dma((nz, nx)), dma((nz,)), dma((nz,)),
        ],
        compiler_params=pltpu.CompilerParams(
            collective_id=0, has_side_effects=True, vmem_limit_bytes=56 << 20
        ),
    )(patches, modality.reshape(1, rows), gains, biases, weights, segments, cotangent)


def solution(mesh):
    nx, ny, nz = mesh.shape["gx"], mesh.shape["gy"], mesh.shape["gz"]

    def body(*arrays):
        patches, weights, segments = arrays[0], arrays[4], arrays[5]
        block, columns = weights.shape[1:]
        fits = (
            ny == 2
            and nx > 1
            and nz > 1
            and columns % (2 * HEAD_DIM) == 0
            and block % HEAD_DIM == 0
            and patches.shape[0] % 16 == 0
            and patches.shape[0] * nx % 32 == 0
            and segments.shape == (1, patches.shape[0] * nx)
            and 2 * patches.shape[1] == MODEL_WIDTH
        )
        return in_one_kernel(nx, nz, *arrays) if fits else on_device(*arrays)

    return jax.shard_map(
        body,
        mesh=mesh,
        in_specs=(
            P(("gz", "gx"), "gy"),
            P(("gz", "gx")),
            P(None, "gy"),
            P(None, "gy"),
            P(None, ("gy", "gz"), "gx"),
            P("gz", None),
            P(("gz", "gy"), "gx"),
        ),
        out_specs=(P(("gz", "gy"), "gx"), P(("gz", "gx"), "gy")),
        check_vma=False,
    )
```

```python
import functools

import jax
import jax.numpy as jnp
from jax import lax
from jax.experimental import pallas as pl
from jax.experimental.pallas import tpu as pltpu
from jax.sharding import PartitionSpec as P

MODEL_WIDTH = 6144
HEAD_DIM = 128
CUTS = 4


EPS = 1e-06


def sum_over_width(totals):
    return lax.psum((totals[0], totals[1]), "gy")


def split_sum(partial_value):
    return lax.psum(partial_value, "gy").astype(jnp.float32)


def on_device(patches, modality, gains, biases, weights, segments, cotangent):
    values_f = patches.astype(jnp.float32)
    totals, squares = sum_over_width((jnp.sum(values_f, -1), jnp.sum(values_f * values_f, -1)))
    average = totals / MODEL_WIDTH
    variance = squares / MODEL_WIDTH - average * average
    mean_removed = values_f - average[:, None]
    inverse_deviation = lax.rsqrt(variance + EPS)[:, None]
    standardized_input = mean_removed * inverse_deviation
    levels = jnp.arange(gains.shape[0], dtype=jnp.int32)
    chosen = (modality[:, None] == levels[None, :])[:, :, None]
    gain_per_row = jnp.sum(jnp.where(chosen, gains[None], 0.0), 1)
    bias_per_row = jnp.sum(jnp.where(chosen, biases[None], 0.0), 1)
    layer_normalized = (standardized_input * gain_per_row + bias_per_row).astype(jnp.bfloat16)
    full_weights = lax.all_gather(weights, "gz", axis=1, tiled=True)
    partial_value = jnp.einsum(
        "rd,kdc->rkc",
        lax.all_gather(layer_normalized, "gx", axis=0, tiled=True),
        full_weights,
        preferred_element_type=jnp.float32,
    ).astype(jnp.bfloat16)
    pack_rows = partial_value.shape[0]
    own_rows = pack_rows // lax.axis_size("gy")
    offset = lax.axis_index("gy") * own_rows
    projected = split_sum(partial_value).astype(jnp.bfloat16)
    queries = lax.dynamic_slice_in_dim(projected[:, 0], offset, own_rows, 0)
    keys, values = (projected[:, 1], projected[:, 2])
    columns = full_weights.shape[2]
    head_count = columns // HEAD_DIM
    queries = queries.reshape(own_rows, head_count, HEAD_DIM)
    keys = keys.reshape(pack_rows, head_count, HEAD_DIM)
    values = values.reshape(pack_rows, head_count, HEAD_DIM)
    segment = segments[0]
    segment_query = lax.dynamic_slice_in_dim(segment, offset, own_rows, 0)
    allowed = (segment_query[:, None] == segment[None, :])[None]
    scaling = HEAD_DIM ** (-0.5)
    scores = jnp.einsum("qhd,khd->hqk", queries, keys, preferred_element_type=jnp.float32) * scaling
    exponent = jnp.where(allowed, jnp.exp(scores), 0.0)
    probs = exponent / jnp.sum(exponent, -1, keepdims=True)
    probs_b = probs.astype(jnp.bfloat16)
    attended = (
        jnp.einsum("hqk,khd->qhd", probs_b, values, preferred_element_type=jnp.float32)
        .astype(jnp.bfloat16)
        .reshape(own_rows, columns)
    )
    upstream = cotangent.reshape(own_rows, head_count, HEAD_DIM)
    dprobs = jnp.einsum("qhd,khd->hqk", upstream, values, preferred_element_type=jnp.float32)
    dvalues = jnp.einsum("hqk,qhd->khd", probs_b, upstream, preferred_element_type=jnp.float32)
    dscores = (probs * (dprobs - jnp.sum(probs * dprobs, -1, keepdims=True)) * scaling).astype(
        jnp.bfloat16
    )
    dqueries = jnp.einsum("hqk,khd->qhd", dscores, keys, preferred_element_type=jnp.float32)
    dkeys = jnp.einsum("hqk,qhd->khd", dscores, queries, preferred_element_type=jnp.float32)
    query_block = lax.dynamic_update_slice_in_dim(
        jnp.zeros((pack_rows, head_count, HEAD_DIM), jnp.float32), dqueries, offset, 0
    )
    stacked = (
        jnp.stack([query_block, dkeys, dvalues], 1)
        .reshape(pack_rows, 3, columns)
        .astype(jnp.bfloat16)
    )
    grad_proj = split_sum(stacked).astype(jnp.bfloat16)
    dnormed = lax.psum_scatter(
        jnp.einsum("rkc,kdc->rd", grad_proj, full_weights, preferred_element_type=jnp.float32),
        "gx",
        scatter_dimension=0,
        tiled=True,
    )
    normalized_gradient = dnormed * gain_per_row
    gradient_row_sum, weighted_row_sum = sum_over_width(
        (jnp.sum(normalized_gradient, -1), jnp.sum(normalized_gradient * standardized_input, -1))
    )
    patch_gradient = inverse_deviation * (
        normalized_gradient
        - gradient_row_sum[:, None] / MODEL_WIDTH
        - standardized_input * (weighted_row_sum[:, None] / MODEL_WIDTH)
    )
    return (attended, patch_gradient)


MESH = pl.DeviceIdType.MESH
F32 = dict(preferred_element_type=jnp.float32)


def dot(a, b, da, db):
    return lax.dot_general(a, b, (((da,), (db,)), ((), ())), **F32)


def layer(
    nx, nz, patches, modality, gains, biases, weights, segments, cotangent, attended, gradient,
    held, mixed, xhat, gain, stat_out, stat_in, normed, rows_in, part_out, part_in, grads,
    up, att_out, att_in, y_out, y_in, z_out, z_in,
    local_sem, pair_send, pair_recv, a_send, a_recv, b_send, b_recv, c_send, c_recv,
    p_send, p_recv, g_send, g_recv, h_send, h_recv, y_send, y_recv, z_send, z_recv,
):
    x, y, z = lax.axis_index("gx"), lax.axis_index("gy"), lax.axis_index("gz")
    other = 1 - y
    rows, width = patches.shape
    block, columns = weights.shape[1:]
    share = columns // 2
    length = rows * nx
    half = length // 2
    count = 2 * width
    upper = lax.div(2 * z, nz)
    outward = 1 - 2 * upper
    at_edge = jnp.logical_or(z == 0, z == nz - 1)
    queue = [upper * i + (1 - upper) * (nz - 1 - i) for i in range(nz)]
    cuts = [(c, pl.ds(c * (length // CUTS), length // CUTS)) for c in range(CUTS)]
    sends = []

    def when(condition, action):
        if condition is None:
            action()
        else:
            pl.when(condition)(action)

    def inside(index):
        return jnp.logical_and(index >= 0, index < nz)

    def send(source, target, send_sem, recv_sem, where, condition=None):
        copy = pltpu.make_async_remote_copy(
            src_ref=source, dst_ref=target, send_sem=send_sem, recv_sem=recv_sem,
            device_id=where, device_id_type=MESH,
        )
        when(condition, copy.start)
        sends.append((condition, copy))
        return copy

    def arrived(target, recv_sem, condition=None):
        copy = pltpu.make_async_remote_copy(
            src_ref=target, dst_ref=target, send_sem=local_sem.at[3], recv_sem=recv_sem,
            device_id={"gy": other}, device_id_type=MESH,
        )
        when(condition, copy.wait_recv)

    def along(axis, me, size, step):
        return {axis: lax.rem(me + step + size, size)}

    barrier = pltpu.get_barrier_semaphore()
    pl.semaphore_signal(barrier, inc=1, device_id={"gy": other}, device_id_type=MESH)
    for step in range(1, nx):
        pl.semaphore_signal(barrier, inc=1, device_id=along("gx", x, nx, step), device_id_type=MESH)
    for step in range(1, nz):
        pl.semaphore_signal(barrier, inc=1, device_id=along("gz", z, nz, step), device_id_type=MESH)
    own_columns = pl.ds(pl.multiple_of(y * share, HEAD_DIM), share)
    other_columns = pl.ds(pl.multiple_of(other * share, HEAD_DIM), share)
    keep = pltpu.make_async_copy(weights.at[:, :, own_columns], mixed.at[y], local_sem.at[0])
    keep.start()
    load = pltpu.make_async_copy(weights, held, local_sem.at[1])
    load.start()

    values = patches[...].astype(jnp.float32)
    mine = jnp.sum(values, -1, keepdims=True) / width
    spread = jnp.sum((values - mine) ** 2, -1, keepdims=True)
    lane = lax.broadcasted_iota(jnp.int32, (rows, HEAD_DIM), 1)
    stat_out[0] = jnp.where(lane == 0, mine, spread)
    pl.semaphore_wait(barrier, nx + nz - 1)
    to_pair = {"gy": other}
    first = send(stat_out.at[0], stat_in.at[0], pair_send.at[0], pair_recv.at[0], to_pair)
    swap_w = send(weights.at[:, :, other_columns], mixed.at[y], pair_send.at[1], pair_recv.at[1], to_pair)
    swap_u = send(cotangent.at[:, other_columns], up.at[y], pair_send.at[2], pair_recv.at[2], to_pair)
    up[y] = cotangent[:, own_columns]

    diagonal = lax.broadcasted_iota(jnp.int32, (rows, rows), 0) == lax.broadcasted_iota(jnp.int32, (rows, rows), 1)
    level = jnp.sum(jnp.where(diagonal, modality[...], 0), 1, keepdims=True)
    for part in range(nz):
        cols = slice(part * block, (part + 1) * block)
        chosen = jnp.zeros((rows, block), jnp.float32)
        for index in range(gains.shape[0]):
            chosen = jnp.where(level == index, gains[index:index + 1, cols], chosen)
        gain[:, cols] = chosen
    first.wait_recv()
    theirs = stat_in[0]
    their_mean, their_spread = theirs[:, 0:1], theirs[:, 1:2]
    average = (mine + their_mean) * 0.5
    variance = (spread + their_spread + (mine - their_mean) ** 2 * (width * 0.5)) / count
    inverse = lax.rsqrt(variance + EPS)
    for part in range(nz):
        cols = slice(part * block, (part + 1) * block)
        offset = jnp.zeros((rows, block), jnp.float32)
        for index in range(biases.shape[0]):
            offset = jnp.where(level == index, biases[index:index + 1, cols], offset)
        standard = (patches[:, cols].astype(jnp.float32) - average) * inverse
        xhat[:, cols] = standard
        normed[part] = (standard * gain[:, cols] + offset).astype(jnp.bfloat16)

    place = pltpu.make_async_copy(normed.at[z], rows_in.at[y, z, x], local_sem.at[2])
    place.start()
    for q in queue:
        send(
            normed.at[q], rows_in.at[y, z, x], a_send.at[q], a_recv.at[z], {"gz": q}, q != z
        )
    for e in range(1, nx):
        send(normed.at[z], rows_in.at[y, z, x], b_send.at[z, e], b_recv.at[z, e], along("gx", x, nx, e))
    for p in queue:
        arrived(rows_in.at[y, p, x], a_recv.at[p], p != z)
        for e in range(1, nx):
            send(
                rows_in.at[y, p, x], rows_in.at[y, p, x], b_send.at[p, e], b_recv.at[p, e],
                along("gx", x, nx, e), p != z,
            )
    place.wait()
    keep.wait()

    def project(p):
        arrived(rows_in.at[other, p], c_recv.at[p])
        for k in range(3):
            total = jnp.zeros((length, share), jnp.float32)
            for g in range(2):
                total = total + dot(rows_in[g, p].reshape(length, block), mixed[g, k], 1, 0)
            part_out[p, :, k * share:(k + 1) * share] = total.astype(jnp.bfloat16)
        for c, cut in cuts:
            send(
                part_out.at[p, cut], part_in.at[upper, p, cut], p_send.at[p, c], p_recv.at[upper, p, c],
                along("gz", z, nz, outward), jnp.logical_and(at_edge, p != z),
            )

    last = None
    for p in queue:
        for e in range(1, nx):
            arrived(rows_in.at[y, p, lax.rem(x - e + nx, nx)], b_recv.at[p, e])
        send(rows_in.at[y, p], rows_in.at[y, p], c_send.at[p], c_recv.at[p], to_pair)
        if last is None:
            swap_w.wait_recv()
        else:
            project(last)
        last = p
    project(last)

    def add_in(side, p, cut):
        total = part_out[p, cut].astype(jnp.float32) + part_in[side, p, cut].astype(jnp.float32)
        part_out[p, cut] = total.astype(jnp.bfloat16)

    for t in range(nz - 1):
        for way in (outward, -outward):
            side = lax.div(1 - way, 2)
            p = (1 - side) * (nz - 1 - t) + side * t
            relays = jnp.logical_and((p - z) * way > 0, inside(z - way))
            for c, cut in cuts:
                arrived(part_in.at[side, p, cut], p_recv.at[side, p, c], relays)
                when(relays, functools.partial(add_in, side, p, cut))
                send(
                    part_out.at[p, cut], part_in.at[side, p, cut], p_send.at[p, c], p_recv.at[side, p, c],
                    along("gz", z, nz, way), relays,
                )

    marks = segments[...]
    diagonal = lax.broadcasted_iota(jnp.int32, (length, length), 0) == lax.broadcasted_iota(
        jnp.int32, (length, length), 1
    )
    allowed = jnp.sum(jnp.where(diagonal, marks, 0), 1, keepdims=True) == marks
    scaling = HEAD_DIM ** (-0.5)
    load.wait()
    swap_u.wait_recv()
    for side, present in ((0, z > 0), (1, z < nz - 1)):
        for c, cut in cuts:
            arrived(part_in.at[side, z, cut], p_recv.at[side, z, c], present)
            when(present, functools.partial(add_in, side, z, cut))
    for h in range(share // HEAD_DIM):
        taken = []
        for k in range(3):
            cols = slice(k * share + h * HEAD_DIM, k * share + (h + 1) * HEAD_DIM)
            taken.append(part_out[z, :, cols])
        query, key, value = taken
        here = slice(h * HEAD_DIM, (h + 1) * HEAD_DIM)
        above = up[:, :, here].reshape(length, HEAD_DIM)
        exponent = jnp.where(allowed, jnp.exp(dot(query, key, 1, 1) * scaling), 0.0)
        probs = exponent / jnp.sum(exponent, -1, keepdims=True)
        probs_b = probs.astype(jnp.bfloat16)
        att = dot(probs_b, value, 1, 0).astype(jnp.bfloat16)
        att_out[:, :, here] = att.reshape(2, half, HEAD_DIM)
        dprobs = dot(above, value, 1, 1)
        dscores = probs * (dprobs - jnp.sum(probs * dprobs, -1, keepdims=True)) * scaling
        dscores_b = dscores.astype(jnp.bfloat16)
        found = (
            dot(dscores_b, key, 1, 0),
            dot(dscores_b, query, 0, 0),
            dot(probs_b, above, 0, 0),
        )
        for k in range(3):
            cols = slice(k * share + h * HEAD_DIM, k * share + (h + 1) * HEAD_DIM)
            grads[z, y, :, cols] = found[k].astype(jnp.bfloat16)

    def pass_on(p, way, condition, c, cut):
        send(
            grads.at[p, y, cut], grads.at[p, y, cut], g_send.at[(1 - way) // 2, p, c], g_recv.at[p, c],
            along("gz", z, nz, way), jnp.logical_and(condition, inside(z + way)),
        )

    for c, cut in cuts:
        for way in (1, -1):
            pass_on(z, way, True, c, cut)
        send(grads.at[z, y, cut], grads.at[z, y, cut], h_send.at[z, c], h_recv.at[z, c], to_pair)
    swap_a = send(att_out.at[other], att_in, pair_send.at[3], pair_recv.at[3], to_pair)

    def back(p, condition=None):
        for c, cut in cuts:
            arrived(grads.at[p, other, cut], h_recv.at[p, c], condition)

        def multiply():
            total = jnp.zeros((length, block), jnp.float32)
            for k in range(3):
                for g in range(2):
                    total = total + dot(
                        grads[p, g, :, k * share:(k + 1) * share], held[k, :, g * share:(g + 1) * share], 1, 1
                    )
            y_out[p] = total.astype(jnp.bfloat16).reshape(nx, rows, block)

        when(condition, multiply)
        for e in range(1, nx):
            send(
                y_out.at[p, lax.rem(x + e, nx)], y_in.at[p, e], y_send.at[p, e], y_recv.at[p, e],
                along("gx", x, nx, e), condition,
            )

    def collect(p, condition=None):
        for e in range(1, nx):
            arrived(y_in.at[p, e], y_recv.at[p, e], condition)

        def add_up():
            total = y_out[p, x].astype(jnp.float32)
            for e in range(1, nx):
                total = total + y_in[p, e].astype(jnp.float32)
            if condition is None:
                z_in[z] = total.astype(jnp.bfloat16)
            else:
                z_out[p] = total.astype(jnp.bfloat16)

        when(condition, add_up)
        if condition is not None:
            send(z_out.at[p], z_in.at[z], z_send.at[p], z_recv.at[z], {"gz": p}, condition)

    back(z)
    attended[:, own_columns] = att_out[y]
    swap_a.wait_recv()
    attended[:, other_columns] = att_in[...]
    waiting = [(z, None)]
    for t in range(1, nz):
        found = []
        for c, cut in cuts:
            for way in (1, -1):
                p = lax.rem(z - way * t + nz, nz)
                present = inside(z - way * t)
                arrived(grads.at[p, y, cut], g_recv.at[p, c], present)
                pass_on(p, way, present, c, cut)
                send(
                    grads.at[p, y, cut], grads.at[p, y, cut], h_send.at[p, c], h_recv.at[p, c], to_pair, present
                )
                if c == 0:
                    found.append((p, present))
        for p, present in waiting:
            collect(p, present)
        for p, present in found:
            back(p, present)
        waiting = found
    for p, present in waiting:
        collect(p, present)

    plain = jnp.zeros((rows, 1), jnp.float32)
    weighted = jnp.zeros((rows, 1), jnp.float32)
    for part in range(nz):
        arrived(z_in.at[part], z_recv.at[part], z != part)
        cols = slice(part * block, (part + 1) * block)
        dxhat = z_in[part].astype(jnp.float32) * gain[:, cols]
        gain[:, cols] = dxhat
        plain = plain + jnp.sum(dxhat, -1, keepdims=True)
        weighted = weighted + jnp.sum(dxhat * xhat[:, cols], -1, keepdims=True)
    stat_out[1] = jnp.where(lane == 0, plain, weighted)
    second = send(stat_out.at[1], stat_in.at[1], pair_send.at[4], pair_recv.at[4], to_pair)
    second.wait_recv()
    theirs = stat_in[1]
    plain = (plain + theirs[:, 0:1]) / count
    weighted = (weighted + theirs[:, 1:2]) / count
    for part in range(nz):
        cols = slice(part * block, (part + 1) * block)
        gradient[:, cols] = inverse * (gain[:, cols] - plain - xhat[:, cols] * weighted)
    for condition, copy in sends:
        when(condition, copy.wait_send)


def in_one_kernel(nx, nz, patches, modality, gains, biases, weights, segments, cotangent):
    rows, width = patches.shape
    block, columns = weights.shape[1:]
    share, length = columns // 2, rows * nx
    half = length // 2
    bf16, f32 = jnp.bfloat16, jnp.float32
    dma = pltpu.SemaphoreType.DMA
    vmem = pl.BlockSpec(memory_space=pltpu.VMEM)
    in_specs = [vmem] * 7
    in_specs[4] = pl.BlockSpec(memory_space=pl.ANY)
    return pl.pallas_call(
        functools.partial(layer, nx, nz),
        out_shape=(
            jax.ShapeDtypeStruct((half, columns), bf16),
            jax.ShapeDtypeStruct((rows, width), f32),
        ),
        in_specs=in_specs,
        out_specs=(vmem, vmem),
        scratch_shapes=[
            pltpu.VMEM((3, block, columns), bf16),
            pltpu.VMEM((2, 3, block, share), bf16),
            pltpu.VMEM((rows, width), f32),
            pltpu.VMEM((rows, width), f32),
            pltpu.VMEM((2, rows, HEAD_DIM), f32),
            pltpu.VMEM((2, rows, HEAD_DIM), f32),
            pltpu.VMEM((nz, rows, block), bf16),
            pltpu.VMEM((2, nz, nx, rows, block), bf16),
            pltpu.VMEM((nz, length, 3 * share), bf16),
            pltpu.VMEM((2, nz, length, 3 * share), bf16),
            pltpu.VMEM((nz, 2, length, 3 * share), bf16),
            pltpu.VMEM((2, half, share), bf16),
            pltpu.VMEM((2, half, share), bf16),
            pltpu.VMEM((half, share), bf16),
            pltpu.VMEM((nz, nx, rows, block), bf16),
            pltpu.VMEM((nz, nx, rows, block), bf16),
            pltpu.VMEM((nz, rows, block), bf16),
            pltpu.VMEM((nz, rows, block), bf16),
            dma((4,)), dma((5,)), dma((5,)), dma((nz,)), dma((nz,)), dma((nz, nx)), dma((nz, nx)),
            dma((nz,)), dma((nz,)), dma((nz, CUTS)), dma((2, nz, CUTS)), dma((2, nz, CUTS)), dma((nz, CUTS)),
            dma((nz, CUTS)), dma((nz, CUTS)),
            dma((nz, nx)), dma((nz, nx)), dma((nz,)), dma((nz,)),
        ],
        compiler_params=pltpu.CompilerParams(
            collective_id=0, has_side_effects=True, vmem_limit_bytes=56 << 20
        ),
    )(patches, modality.reshape(1, rows), gains, biases, weights, segments, cotangent)


def solution(mesh):
    nx, ny, nz = mesh.shape["gx"], mesh.shape["gy"], mesh.shape["gz"]

    def body(*arrays):
        patches, weights, segments = arrays[0], arrays[4], arrays[5]
        block, columns = weights.shape[1:]
        fits = (
            ny == 2
            and nx > 1
            and nz > 1
            and columns % (2 * HEAD_DIM) == 0
            and block % HEAD_DIM == 0
            and patches.shape[0] % 16 == 0
            and patches.shape[0] * nx % (16 * CUTS) == 0
            and segments.shape == (1, patches.shape[0] * nx)
            and 2 * patches.shape[1] == MODEL_WIDTH
        )
        return in_one_kernel(nx, nz, *arrays) if fits else on_device(*arrays)

    return jax.shard_map(
        body,
        mesh=mesh,
        in_specs=(
            P(("gz", "gx"), "gy"),
            P(("gz", "gx")),
            P(None, "gy"),
            P(None, "gy"),
            P(None, ("gy", "gz"), "gx"),
            P("gz", None),
            P(("gz", "gy"), "gx"),
        ),
        out_specs=(P(("gz", "gy"), "gx"), P(("gz", "gx"), "gy")),
        check_vma=False,
    )
```
